32 devices in a mesh: seq: 4 (over z), head: 8 (over y, x, core).
Axes of the slice: x: 2, y: 2, z: 4, core: 2. Of those that a mesh axis runs over, the one named last changes fastest.
Arguments:
- x_in: bfloat16 [2048, 8192], P('seq', 'head'), may hold values from -6 to 6
- z_in: bfloat16 [2048, 8192], P('seq', 'head'), may hold values from -6 to 6
- bc_in: bfloat16 [2048, 2048], P('seq'), may hold values from -6 to 6
- conv_x: float32 [4, 8192], P(None, 'head'), may hold values from -3 to 3
- conv_bc: float32 [4, 2048], replicated, may hold values from -3 to 3
- dt: float32 [128, 2048], P('head', 'seq'), may hold values from 0 to 3, as said below
- a_log: float32 [128], P('head'), may hold values from -2 to 1, as said below
- skip_d: float32 [128], P('head'), may hold values from 0.5 to 1.5
- norm_gain: float32 [8192], P('head'), may hold values from 0.5 to 1.5
- seg_ids: int32 [2048], P('seq'), may hold values from 0 to 3, as said below
Outputs:
- mixed: bfloat16 [2048, 8192], P('seq', 'head')
The draws below stay inside these ranges and needn't reach their ends.
Inputs may be any that keep to these rules, and one draw needn't show every extreme that they name: `a_log`: log of a decay rate of order one. `dt`: positive step sizes. `seg_ids`: document numbers never fall along the window, every document is nonempty, and the longest document holds exactly 1024 tokens.
All inputs are finite; a program needn't handle non-finite values.
Results may differ from the reference program's by a relative error of at most 0.0051.
Values may be sent and summed in bfloat16 or wider, within the bound.
No kernel may reach another device: no remote copies, remote signals or barrier semaphores. Data moves between devices by JAX's collectives and lax.ppermute only.
A program may use at most 64 MiB of HBM per device.

```python
import math
import jax
import jax.numpy as jnp
from jax import lax

HEADS = 128
HEAD_DIM = 64
STATE = 128
GROUPS = 8
KERNEL = 4
SPAN = 128
TOK_DEV = 512
INNER = 8192
TOKENS = 2048


def decay_parts(key):
    base = jax.random.fold_in(key, 7)
    keys = jax.random.split(base, 5)
    share = 0.5
    slow = jax.random.uniform(keys[0], (HEADS,)) < share
    slow_rate = jnp.exp(jax.random.uniform(keys[1], (HEADS,), minval=math.log(0.5), maxval=math.log(2.0)))
    fast_rate = jnp.exp(jax.random.uniform(keys[2], (HEADS,), minval=math.log(0.15), maxval=math.log(0.4)))
    decay_matrix = jnp.where(slow, slow_rate, fast_rate)
    slow_step = jnp.exp(jax.random.uniform(keys[3], (HEADS,), minval=math.log(0.25 / TOKENS), maxval=math.log(1.2 / TOKENS)))
    fast_step = jnp.exp(jax.random.uniform(keys[4], (HEADS,), minval=math.log(1.0 / 50.0), maxval=math.log(1.0 / 25.0)))
    per_step = jnp.where(slow, slow_step, fast_step)
    return (decay_matrix, per_step)


def draw_a_log(key, part):
    decay_matrix, per_step = decay_parts(key)
    return jnp.log(decay_matrix).astype(jnp.float32)


def draw_dt(key, part):
    decay_matrix, per_step = decay_parts(key)
    keys = jax.random.split(jax.random.fold_in(key, 11), 3)
    rough = jnp.exp(jax.random.uniform(keys[0], (HEADS, TOKENS), minval=math.log(0.5), maxval=math.log(2.0)))
    step_sizes = per_step[:, None] / decay_matrix[:, None] * rough
    places = jax.random.randint(keys[1], (6,), 0, TOKENS)
    match_flags = jnp.any(jnp.arange(TOKENS)[None, :] == places[:, None], axis=0)
    objective_value = jax.random.uniform(keys[2], (HEADS, TOKENS), minval=0.2, maxval=0.4)
    step_increment = objective_value / decay_matrix[:, None]
    step_sizes = jnp.where(match_flags[None, :], jnp.maximum(step_sizes, step_increment), step_sizes)
    return step_sizes.astype(jnp.float32)


def draw_seg_ids(key, part):
    keys = jax.random.split(jax.random.fold_in(key, 23), 2)
    long_start = TOKENS // 4 + jax.random.randint(keys[0], (), 1, TOK_DEV)
    first_end = jax.random.randint(keys[1], (), 1, long_start)
    long_end = long_start + TOKENS // 2
    position = jnp.arange(TOKENS, dtype=jnp.int32)
    doc_number = (position >= first_end).astype(jnp.int32) + (position >= long_start).astype(jnp.int32) + (position >= long_end).astype(jnp.int32)
    return doc_number.astype(jnp.int32)


def shard_levels(stream_key, dims, shards, smallest, largest):
    def one(axis_at, shards_of):
        heights = jax.random.uniform(jax.random.fold_in(jax.random.fold_in(stream_key, 6), axis_at), (shards_of,), jnp.float32, smallest / len(shards), largest / len(shards))
        return jnp.repeat(jnp.exp(heights), dims[axis_at] // shards_of).reshape((-1,) + (1,) * (len(dims) - axis_at - 1))

    factor_of = one(*shards[0])
    for cut in shards[1:]:
        factor_of = factor_of * one(*cut)
    return factor_of


def gaussian(key, shape, deviation, limit, cuts=(), held_as=jnp.bfloat16):
    values = deviation * jax.random.normal(key, shape, jnp.float32)
    if cuts:
        values = values * shard_levels(key, shape, cuts, -0.22, 0.18)
    return jnp.clip(values, -limit, limit).astype(held_as)


def setup_inputs(seed: int = 0) -> dict:
    arg_keys = jax.random.split(jax.random.key(seed), 11)
    x_in = gaussian(arg_keys[0], (TOKENS, INNER), 1.0, 6.0, ((0, 4), (1, 8)))
    z_in = gaussian(arg_keys[1], (TOKENS, INNER), 1.0, 6.0, ((0, 4), (1, 8)))
    bc_in = gaussian(arg_keys[2], (TOKENS, 2 * GROUPS * STATE), 1.0, 6.0, ((0, 4),))
    conv_x = gaussian(arg_keys[3], (KERNEL, INNER), KERNEL ** -0.5, 3.0, ((1, 8),), jnp.float32)
    conv_bc = gaussian(arg_keys[4], (KERNEL, 2 * GROUPS * STATE), KERNEL ** -0.5, 3.0, (), jnp.float32)
    dt = draw_dt(jax.random.fold_in(arg_keys[10], 71), 0)
    a_log = draw_a_log(jax.random.fold_in(arg_keys[10], 71), 0)
    skip_d = jnp.clip(0.5 + 1.0 * jax.random.uniform(arg_keys[7], (HEADS,), jnp.float32) ** shard_levels(arg_keys[7], (HEADS,), ((0, 8),), -0.2, 0.2), 0.5, 1.5)
    norm_gain = jnp.clip(1.0 + 0.1 * jax.random.normal(arg_keys[8], (INNER,), jnp.float32), 0.5, 1.5)
    seg_ids = draw_seg_ids(jax.random.fold_in(arg_keys[10], 71), 0)
    return {"x_in": x_in, "z_in": z_in, "bc_in": bc_in, "conv_x": conv_x, "conv_bc": conv_bc, "dt": dt, "a_log": a_log, "skip_d": skip_d, "norm_gain": norm_gain, "seg_ids": seg_ids}


def conv_silu(data, weight, seg_ids):
    rows = data.shape[0]
    width = data.shape[1]
    padded = jnp.concatenate([jnp.zeros((KERNEL - 1, width), jnp.bfloat16), data], 0)
    seg_pad = jnp.concatenate([jnp.full((KERNEL - 1,), -1, jnp.int32), seg_ids.astype(jnp.int32)], 0)
    total = jnp.zeros((rows, width), jnp.float32)
    for offset in range(KERNEL):
        window = padded[offset:offset + rows].astype(jnp.float32)
        same_doc = (seg_pad[offset:offset + rows] == seg_ids)[:, None]
        total = total + jnp.where(same_doc, window, 0.0) * weight[offset]
    return jax.nn.silu(total).astype(jnp.bfloat16)

def reference(x_in, z_in, bc_in, conv_x, conv_bc, dt, a_log, skip_d, norm_gain, seg_ids):
    x_conv = conv_silu(x_in, conv_x, seg_ids)
    bc_conv = conv_silu(bc_in, conv_bc, seg_ids)
    per_group = HEADS // GROUPS
    spans = TOKENS // SPAN
    x_blocks = x_conv.reshape(spans, SPAN, HEADS, HEAD_DIM)
    b_blocks = bc_conv[:, :GROUPS * STATE].reshape(spans, SPAN, GROUPS, STATE)
    c_blocks = bc_conv[:, GROUPS * STATE:].reshape(spans, SPAN, GROUPS, STATE)
    dt_blocks = dt.reshape(HEADS, spans, SPAN).transpose(1, 0, 2)
    seg_blocks = seg_ids.reshape(spans, SPAN)
    seg_before = jnp.concatenate([jnp.full((1,), -1, jnp.int32), seg_blocks[:-1, -1].astype(jnp.int32)])
    rates = jnp.exp(a_log)
    causal = jnp.tril(jnp.ones((SPAN, SPAN), bool))

    def advance(state, inputs):
        x_blk, b_blk, c_blk, dt_blk, seg_blk, seg_prev = inputs
        log_decay = jnp.cumsum(-dt_blk * rates[:, None], axis=1)
        same_doc = ((seg_blk[:, None] == seg_blk[None, :]) & causal)[None]
        spread = log_decay[:, :, None] - log_decay[:, None, :]
        decay = jnp.where(same_doc, jnp.exp(jnp.where(same_doc, spread, 0.0)), 0.0)
        scores = jnp.einsum('tgn,sgn->gts', c_blk.astype(jnp.float32), b_blk.astype(jnp.float32))
        scores = jnp.repeat(scores, per_group, axis=0)
        weight_tensors = (scores * decay * dt_blk[:, None, :]).astype(jnp.bfloat16)
        y_diag = jnp.einsum('hts,shp->thp', weight_tensors.astype(jnp.float32), x_blk.astype(jnp.float32))
        alive = (seg_blk == seg_prev).astype(jnp.float32)
        c_heads = jnp.repeat(c_blk, per_group, axis=1).astype(jnp.float32)
        y_carry = jnp.einsum('thn,hpn->thp', c_heads, state, precision=lax.Precision.HIGHEST)
        y_carry = y_carry * (jnp.exp(log_decay).T * alive[:, None])[:, :, None]
        to_end = jnp.exp(log_decay[:, -1:] - log_decay) * dt_blk * (seg_blk == seg_blk[-1]).astype(jnp.float32)[None, :]
        x_weighted = (x_blk.astype(jnp.float32) * to_end.T[:, :, None]).astype(jnp.bfloat16)
        b_heads = jnp.repeat(b_blk, per_group, axis=1).astype(jnp.float32)
        fresh = jnp.einsum('shp,shn->hpn', x_weighted.astype(jnp.float32), b_heads)
        keep = jnp.exp(log_decay[:, -1]) * (seg_blk[-1] == seg_prev).astype(jnp.float32)
        return (keep[:, None, None] * state + fresh, y_diag + y_carry)
    start = jnp.zeros((HEADS, HEAD_DIM, STATE), jnp.float32)
    _, y_blocks = lax.scan(advance, start, (x_blocks, b_blocks, c_blocks, dt_blocks, seg_blocks, seg_before))
    summed = y_blocks.reshape(TOKENS, HEADS, HEAD_DIM) + skip_d[None, :, None] * x_conv.reshape(TOKENS, HEADS, HEAD_DIM).astype(jnp.float32)
    gated = summed * jax.nn.silu(z_in.reshape(TOKENS, HEADS, HEAD_DIM).astype(jnp.float32))
    flat = gated.reshape(TOKENS, INNER)
    mean_sq = lax.optimization_barrier(jnp.mean(flat * flat, axis=1, keepdims=True))
    normalized_output = flat * lax.rsqrt(mean_sq + 1e-05)
    return (normalized_output * norm_gain).astype(jnp.bfloat16)
```

```python
import functools
import jax
import jax.numpy as jnp
from jax import lax
from jax.experimental import pallas as pl
from jax.experimental.pallas import tpu as pltpu
from jax.sharding import PartitionSpec as P

HEADS = 128
HEAD_DIM = 64
STATE = 128
GROUPS = 8
KERNEL = 4
SPAN = 128
LOG2E = 1.4426950408889634
TINY = 1e-37
TAIL = 16
f32 = jnp.float32
bf16 = jnp.bfloat16


def mm(a, b, ca=1, cb=0):
    return lax.dot_general(a, b, (((ca,), (cb,)), ((), ())), preferred_element_type=f32)


def iota(shape, axis):
    return lax.broadcasted_iota(jnp.int32, shape, axis)


def split(value, parts):
    pieces = []
    for _ in range(parts):
        piece = value.astype(bf16)
        pieces.append(piece)
        value = value - piece.astype(f32)
    return jnp.concatenate(pieces, 0)


def expander(heads, parts, width, first):
    row = iota((parts * heads, width), 0) & (heads - 1)
    col = (iota((parts * heads, width), 1) >> 6) + first
    return jnp.where(row == col, 1.0, 0.0).astype(bf16)


def silu_from_half(half):
    return half + half * jnp.tanh(half)


def blk(b):
    return slice(b * SPAN, (b + 1) * SPAN)


def to_column(row):
    n = row.shape[1]
    rows = jnp.where(iota((16, n), 0) == 0, row, 0.0).astype(bf16)
    return mm(rows, jnp.ones((16, 128), bf16), 0, 0)


def chunk_state(hp, first, x, taps, shift, bt, rows, kcols, drop, xc, lstate, krows, msg):
    tokens, wc = x.shape
    nb = tokens // SPAN
    kr = mm(split(kcols, 3), expander(hp, 3, wc, first), 0, 0)[:16]
    krows[...] = kr
    tile = 256 if wc % 256 == 0 else wc
    ex = expander(hp, 2, wc, first)
    for j in range(wc // tile):
        js = slice(j * tile, (j + 1) * tile)
        state = None
        for b in range(nb):
            if b == 0:
                sh = mm(shift[0 : 3 * SPAN, SPAN:], x[blk(0), js])
            else:
                sh = mm(
                    shift[3 * SPAN * b : 3 * SPAN * (b + 1), :],
                    x[(b - 1) * SPAN : (b + 1) * SPAN, js],
                )
            half = sh[0:SPAN] * taps[0:1, js] + sh[SPAN : 2 * SPAN] * taps[1:2, js]
            half = half + sh[2 * SPAN :] * taps[2:3, js]
            half = half + x[blk(b), js].astype(f32) * taps[3:4, js]
            act = silu_from_half(half)
            if b == 0:
                act = jnp.where(iota(act.shape, 0).astype(f32) < drop, 0.0, act)
            act = act.astype(bf16)
            xc[blk(b), js] = act
            to_end = mm(split(rows[3 * hp : 4 * hp, blk(b)], 2), ex[:, js], 0, 0)
            weighted = (act.astype(f32) * to_end).astype(bf16)
            fresh = mm(bt[:, blk(b)], weighted)
            state = fresh if b == 0 else state * kr[b : b + 1, js] + fresh
            if b < nb - 1:
                hi = state.astype(bf16)
                lstate[2 * SPAN * b : 2 * SPAN * b + SPAN, js] = hi
                lstate[2 * SPAN * b + SPAN : 2 * SPAN * (b + 1), js] = (
                    state - hi.astype(f32)
                ).astype(bf16)
        msg[0:STATE, js] = state.astype(bf16)


def first_kernel(
    heads, hp, nch,
    x_any, bc_any, tapbc_any, tapx, dt_ref, alog_ref, skip_ref, seg_ref,
    msg, xc, lstate, krows, bcc, bt, rows, kcols, shift, xhead, bchead, taps_bc,
    xbuf, bcbuf, xtail, sems,
):
    tokens, wc = xbuf.shape
    nb = tokens // SPAN
    group = lax.axis_index("head") * heads // (HEADS // GROUPS)
    col_b = pl.multiple_of(group * STATE, STATE)
    col_c = pl.multiple_of((group + GROUPS) * STATE, STATE)
    width = nch * wc
    copies = [
        pltpu.make_async_copy(bc_any.at[:, pl.ds(col_b, STATE)], bcbuf.at[:, 0:STATE], sems.at[0]),
        pltpu.make_async_copy(bc_any.at[:, pl.ds(col_c, STATE)], bcbuf.at[:, STATE:], sems.at[1]),
        pltpu.make_async_copy(tapbc_any.at[:, pl.ds(col_b, STATE)], taps_bc.at[:, 0:STATE], sems.at[2]),
        pltpu.make_async_copy(tapbc_any.at[:, pl.ds(col_c, STATE)], taps_bc.at[:, STATE:], sems.at[3]),
        pltpu.make_async_copy(x_any.at[:, 0:wc], xbuf, sems.at[4]),
        pltpu.make_async_copy(x_any.at[tokens - TAIL :, :], xtail, sems.at[5]),
        pltpu.make_async_copy(x_any.at[0:TAIL, :], xhead, sems.at[6]),
    ]
    for copy in copies:
        copy.start()
    seg = seg_ref[...].astype(f32)
    seg_first = seg[:, 0:1]
    seg_last = [seg[:, (b + 1) * SPAN - 1 : (b + 1) * SPAN] for b in range(nb)]
    eye = iota((hp, hp), 0) == iota((hp, hp), 1)
    rate = jnp.exp(jnp.sum(jnp.where(eye, alog_ref[...], 0.0), axis=1, keepdims=True))
    skip = jnp.sum(jnp.where(eye, skip_ref[...], 0.0), axis=1, keepdims=True)
    dt = dt_ref[...]
    parts = split(dt * (rate * -LOG2E), 3)
    tri = jnp.where(iota((SPAN, SPAN), 0) <= iota((SPAN, SPAN), 1), 1.0, 0.0).astype(bf16)
    sums = mm(jnp.concatenate([parts[:, blk(b)] for b in range(nb)], 0), tri)
    lane = iota((hp, SPAN), 1)
    lane1 = iota((1, SPAN), 1)
    before = jnp.zeros((hp, 1), f32)
    kc = jnp.where(lane == 11, skip, 0.0)
    for b in range(nb):
        three = sums[3 * hp * b : 3 * hp * (b + 1)]
        cum = three[0:hp] + three[hp : 2 * hp] + three[2 * hp :]
        last = cum[:, SPAN - 1 : SPAN]
        segb, dtb = seg[:, blk(b)], dt[:, blk(b)]
        total = cum + before
        rows[0:hp, blk(b)] = cum
        rows[hp : 2 * hp, blk(b)] = jnp.exp2(total) * jnp.where(segb == seg_first, 1.0, 0.0)
        if b > 0:
            rows[2 * hp : 3 * hp, blk(b)] = jnp.exp2(cum) * jnp.where(segb == seg_last[b - 1], 1.0, 0.0)
            keep = jnp.exp2(last) * jnp.where(seg_last[b] == seg_last[b - 1], 1.0, 0.0)
            kc = kc + jnp.where(lane == b, keep, 0.0)
        else:
            rows[2 * hp : 3 * hp, blk(b)] = jnp.zeros((hp, SPAN), f32)
            is_drop = jnp.where((lane1 < KERNEL - 1) & (segb == seg_first), 1.0, 0.0)
            drop = jnp.sum(is_drop, axis=1, keepdims=True)
            early = jnp.exp2(jnp.where(lane < KERNEL - 1, -cum, 0.0)) * dtb * is_drop
            kc = kc + pltpu.roll(early, 8, 1)
        rows[3 * hp : 4 * hp, blk(b)] = jnp.exp2(last - cum) * dtb * jnp.where(segb == seg_last[b], 1.0, 0.0)
        rows[4 * hp : 5 * hp, blk(b)] = cum - jnp.log2(jnp.maximum(dtb, TINY))
        before = before + last
    fend = jnp.exp2(before) * jnp.where(seg_last[-1] == seg_first, 1.0, 0.0)
    kc = kc + jnp.where(lane == 0, fend, 0.0) + jnp.where(lane == 16, drop, 0.0)
    kcols[...] = kc
    delta = iota((SPAN, SPAN), 1) - iota((SPAN, SPAN), 0)
    for b in range(nb):
        segcol = to_column(seg[:, blk(b)])
        same = segcol == seg[:, blk(b)]
        for k in range(KERNEL - 1):
            back = KERNEL - 1 - k
            r = slice(3 * SPAN * b + SPAN * k, 3 * SPAN * b + SPAN * (k + 1))
            shift[r, SPAN:] = jnp.where((delta == -back) & same, 1.0, 0.0).astype(bf16)
            if b > 0:
                same_prev = segcol == seg[:, blk(b - 1)]
                shift[r, 0:SPAN] = jnp.where((delta == SPAN - back) & same_prev, 1.0, 0.0).astype(bf16)
            else:
                shift[r, 0:SPAN] = jnp.zeros((SPAN, SPAN), bf16)
    for copy in copies[:4]:
        copy.wait()
    bchead[...] = bcbuf[0:TAIL, :]
    tb = taps_bc[...] * 0.5
    for b in range(nb):
        if b == 0:
            sh = mm(shift[0 : 3 * SPAN, SPAN:], bcbuf[blk(0), :])
        else:
            sh = mm(shift[3 * SPAN * b : 3 * SPAN * (b + 1), :], bcbuf[(b - 1) * SPAN : (b + 1) * SPAN, :])
        half = sh[0:SPAN] * tb[0:1] + sh[SPAN : 2 * SPAN] * tb[1:2]
        half = half + sh[2 * SPAN :] * tb[2:3] + bcbuf[blk(b), :].astype(f32) * tb[3:4]
        act = silu_from_half(half).astype(bf16)
        bcc[blk(b), :] = act
        bt[:, blk(b)] = act[:, 0:STATE].T
    for copy in copies[4:]:
        copy.wait()
    chunk_state(
        hp, 0, xbuf, tapx[:, 0:wc] * 0.5, shift, bt, rows, kc, drop, xc, lstate, krows, msg
    )
    lane_last = iota((1, SPAN), 1)
    is_tail = jnp.where((lane_last >= SPAN - (KERNEL - 1)) & (seg[:, blk(nb - 1)] == seg_last[-1]), 1.0, 0.0)
    first_valid = 8.0 - jnp.sum(is_tail, axis=1, keepdims=True)

    def tail_of(value):
        rows8 = value.astype(f32)[8:16]
        return jnp.where(iota(rows8.shape, 0).astype(f32) >= first_valid, rows8, 0.0)

    tile0 = tail_of(xtail[:, 0:wc])
    if nch == 2:
        tile0 = tile0 + pltpu.roll(tail_of(xtail[:, wc:]), 4, 0)
    tile0 = jnp.where(iota(tile0.shape, 0) == 0, seg_last[-1] + 1.0, tile0)
    tail_bc = tail_of(bcbuf[tokens - TAIL :, :])
    tile1 = tail_bc[:, 0:STATE] + pltpu.roll(tail_bc[:, STATE:], 4, 0)
    if wc > STATE:
        tile1 = jnp.concatenate([tile1, jnp.zeros((8, wc - STATE), f32)], 1)
    msg[STATE:, :] = jnp.concatenate([tile0, tile1], 0).astype(bf16)


def next_kernel(hp, first, x_any, tapx, shift, bt, rows, kcols, msg, xc, lstate, krows, xbuf, sem):
    wc = xbuf.shape[1]
    copy = pltpu.make_async_copy(x_any.at[:, wc : 2 * wc], xbuf, sem)
    copy.start()
    copy.wait()
    chunk_state(
        hp, first, xbuf, tapx[:, wc : 2 * wc] * 0.5, shift, bt, rows, kcols[...],
        kcols[0:1, 16:17], xc, lstate, krows, msg,
    )


def early_conv(halo, head, taps):
    rows = jnp.concatenate([halo, head.astype(f32)[0:8]], 0)
    half = rows[5:13] * taps[0:1]
    for k in range(1, KERNEL):
        half = half + rows[5 + k : 13 + k] * taps[k : k + 1]
    return silu_from_half(half)


def relay_state(krows, recv, b8, xw8, flag):
    base = recv.astype(f32) * flag + mm(b8, xw8, 0, 0)
    return (base * krows[0:1]).astype(bf16)


def relay_first(nch, recv, xhead, bchead, tapx, taps_bc, seg_ref, bcc, *refs):
    krows = refs[:nch]
    out, xw8_ref, x8_ref, b8_ref, c8_ref, flag_ref = refs[nch:]
    wc = out.shape[1]
    tile = recv[STATE:, :].astype(f32)
    tile0, tile1 = tile[0:8], tile[8:16, 0:STATE]
    seg = seg_ref[:, 0:SPAN].astype(f32)
    seg_first = seg[:, 0:1]
    lane = iota((1, SPAN), 1)
    drop = jnp.sum(
        jnp.where((lane < KERNEL - 1) & (seg == seg_first), 1.0, 0.0), axis=1, keepdims=True
    )
    joined = jnp.where(tile0[0:1, 0:1] == seg_first + 1.0, 1.0, 0.0)
    flag = joined * jnp.where(lax.axis_index("seq") == 0, 0.0, 1.0)
    flag_ref[...] = jnp.broadcast_to(flag, (8, 128))

    def lower(value):
        return jnp.where(iota(value.shape, 0) >= 8 - (KERNEL - 1), value, 0.0) * flag

    def early(value):
        return jnp.where(iota(value.shape, 0).astype(f32) < drop, value, 0.0)

    zero8 = lambda n: jnp.zeros((8, n), f32)
    halo = [lower(tile0)]
    if nch == 2:
        halo.append(lower(pltpu.roll(tile0, 4, 0)))
    bc8 = early_conv(
        jnp.concatenate([lower(tile1), lower(pltpu.roll(tile1, 4, 0))], 1), bchead[...], taps_bc[...] * 0.5
    )
    b8 = jnp.concatenate([early(bc8[:, 0:STATE]), zero8(STATE)], 0).astype(bf16)
    b8_ref[...] = b8
    old = bcc[0:TAIL, STATE:].astype(f32)
    c8 = jnp.where(iota((8, STATE), 0).astype(f32) < drop, bc8[:, STATE:], old[0:8])
    c8_ref[...] = jnp.concatenate([c8, old[8:16]], 0).astype(bf16)
    for c in range(nch):
        cs = slice(c * wc, (c + 1) * wc)
        x8 = early(early_conv(halo[c], xhead[:, cs], tapx[:, cs] * 0.5)).astype(bf16).astype(f32)
        kr = krows[c][...]
        x8_ref[:, cs] = x8 * kr[11:12]
        xw8 = jnp.concatenate([x8 * kr[8:16], zero8(wc)], 0).astype(bf16)
        xw8_ref[:, cs] = xw8
        if c == 0:
            out[...] = relay_state(kr, recv[0:STATE, :], b8, xw8, flag)


def relay_next(recv, krows, b8, xw8, flag, out):
    wc = out.shape[1]
    out[...] = relay_state(krows[...], recv[...], b8[...], xw8[:, wc:], flag[0:1, 0:1])


def local_kernel(hp, first, z_any, xc, lstate, krows, bcc, bt, rows, seg_ref, order, a_ref, q_ref, sz8, zbuf, sem):
    tokens, wc = zbuf.shape
    nb = tokens // SPAN
    lane0 = first * HEAD_DIM
    copy = pltpu.make_async_copy(z_any.at[:, lane0 : lane0 + wc], zbuf, sem)
    copy.start()
    seg = seg_ref[...].astype(f32)
    ex = expander(hp, 2, wc, first)
    r128 = iota((128, SPAN), 0)
    head_of = r128 & (hp - 1)
    low = iota((SPAN, 128), 1) < HEAD_DIM
    tri = iota((SPAN, SPAN), 0) >= iota((SPAN, SPAN), 1)
    waited = False
    for b in range(nb):
        segcol = to_column(seg[:, blk(b)])
        mask = (segcol == seg[:, blk(b)]) & tri
        c_blk = bcc[blk(b), STATE:]
        scores = jnp.where(mask, mm(c_blk, bt[:, blk(b)]), 0.0)
        cum = split(rows[0:hp, blk(b)], 3)
        neg_q = split(-rows[4 * hp : 5 * hp, blk(b)], 3)
        ones = jnp.ones((3 * hp, SPAN), bf16)
        pad = jnp.zeros((128 - 6 * hp, SPAN), bf16)
        left = jnp.concatenate([cum, ones, pad], 0).T
        right = jnp.concatenate([ones, neg_q, pad], 0).astype(f32)
        f_exp = mm(split(rows[hp : 2 * hp, blk(b)], 2), ex, 0, 0)
        if b > 0:
            e_exp = mm(split(rows[2 * hp : 3 * hp, blk(b)], 2), ex, 0, 0)
            carry = mm(
                jnp.concatenate([c_blk, c_blk], 1), lstate[2 * SPAN * (b - 1) : 2 * SPAN * b, :]
            )
        if not waited:
            copy.wait()
            waited = True
        for j in range(wc // 128):
            js = slice(j * 128, (j + 1) * 128)
            xj = xc[blk(b), js]
            w = []
            for i in range(2):
                h = first + 2 * j + i
                sel = jnp.where(head_of == h, right, 0.0).astype(bf16)
                w.append((scores * jnp.exp2(jnp.minimum(mm(left, sel), 8.0))).astype(bf16))
            zero = jnp.zeros_like(xj)
            pair = jnp.concatenate([jnp.where(low, xj, zero), jnp.where(low, zero, xj)], 0)
            y = mm(jnp.concatenate(w, 1), pair) + xj.astype(f32) * krows[11:12, js]
            if b > 0:
                y = y + e_exp[:, js] * carry[:, js]
            sz = silu_from_half(zbuf[blk(b), js].astype(f32) * 0.5)
            a_ref[blk(b), js] = y * sz
            q_ref[blk(b), js] = f_exp[:, js] * sz
            if b == 0:
                sz8[:, js] = sz[0:8]


def rank_kernel(bcc, b8, c8, cg):
    tokens = bcc.shape[0]
    b_pad = jnp.concatenate([b8[...], jnp.zeros((128 - TAIL, STATE), bf16)], 0)
    cg[:, 0:STATE] = bcc[:, STATE:]
    cg[0:TAIL, 0:STATE] = c8[...]
    c = cg[:, 0:STATE]
    cg[:, STATE : 2 * STATE] = c
    g = mm(c, b_pad, 1, 1)
    cg[:, 2 * STATE :] = jnp.where(
        iota((tokens, 128), 0) >= iota((tokens, 128), 1), g, 0.0
    ).astype(bf16)


def gate_kernel(nrecv, chunk, cg, xw8, x8, flag, a_ref, q_ref, sz8, prev, *refs):
    recvs, (gated, sums) = refs[:nrecv], refs[nrecv:]
    tokens, wc = a_ref.shape
    lanes = slice(chunk * wc, (chunk + 1) * wc)
    total = recvs[0][0:STATE, :].astype(f32)
    for r in recvs[1:]:
        total = total + r[0:STATE, :].astype(f32)
    total = total * flag[0:1, 0:1]
    hi = total.astype(bf16)
    lo = (total - hi.astype(f32)).astype(bf16)
    both = jnp.concatenate([hi, lo], 0)
    small = jnp.concatenate([xw8[:, lanes], jnp.zeros((128 - TAIL, wc), bf16)], 0)
    ones = jnp.ones((16, 128), bf16)
    for b in range(tokens // SPAN):
        p = mm(cg[blk(b), 0 : 2 * STATE], both) + mm(cg[blk(b), 2 * STATE :], small)
        g = a_ref[blk(b), :] + q_ref[blk(b), :] * p
        if b == 0:
            top = g[0:8] + x8[:, lanes] * sz8[...]
            g = jnp.concatenate([top, g[8:]], 0)
        gated[blk(b), :] = g
        sq = g * g
        acc = sq[:, 0:128]
        for j in range(1, wc // 128):
            acc = acc + sq[:, j * 128 : (j + 1) * 128]
        acc3 = split(acc, 3)
        s = mm(ones, acc3, 1, 1)
        s = s[0:1, 0:SPAN] + s[0:1, SPAN : 2 * SPAN] + s[0:1, 2 * SPAN :]
        sums[:, blk(b)] = s + prev[:, blk(b)]


def norm_kernel(nch, sums, gain, *refs):
    gated, out = refs[:nch], refs[nch]
    wc = gated[0].shape[1]
    b = pl.program_id(0)
    row = pl.ds(pl.multiple_of(b * SPAN, SPAN), SPAN)
    total = jnp.sum(sums[...], axis=0, keepdims=True)
    scale = lax.rsqrt(total / (HEADS * HEAD_DIM) + 1e-05)
    wide = jnp.where(iota((16, SPAN), 0) == 0, scale, 0.0)
    col = mm(split(wide, 3), jnp.ones((48, 128), bf16), 0, 0)
    for c in range(nch):
        for j in range(wc // 128):
            js = slice(j * 128, (j + 1) * 128)
            at = slice(c * wc + j * 128, c * wc + (j + 1) * 128)
            out[:, at] = (gated[c][row, js] * col * gain[:, at]).astype(bf16)


VMEM = pl.BlockSpec(memory_space=pltpu.VMEM)
ANY = pl.BlockSpec(memory_space=pl.ANY)


def call(body, ins, outs, scratch=(), name=None, limit=24 << 20):
    return pl.pallas_call(
        body,
        out_shape=[pltpu.VMEM(shape, dtype) for shape, dtype in outs],
        in_specs=ins,
        out_specs=[VMEM] * len(outs),
        scratch_shapes=list(scratch),
        compiler_params=pltpu.CompilerParams(vmem_limit_bytes=limit),
        name=name,
    )


def per_device(x_in, z_in, bc_in, conv_x, conv_bc, dt, a_log, skip_d, norm_gain, seg_ids):
    tokens, width = x_in.shape
    heads = dt.shape[0]
    nb = tokens // SPAN
    hp = max(16, heads)
    peers = lax.axis_size("seq")
    rounds = max(1, peers // 2)
    nch = 2 if width % 512 == 0 else 1
    wc = width // nch
    per_chunk = heads // nch
    ring = [(i, (i + 1) % peers) for i in range(peers)]
    if hp != heads:
        dt = jnp.pad(dt, ((0, hp - heads), (0, 0)))
        a_log = jnp.pad(a_log, (0, hp - heads))
        skip_d = jnp.pad(skip_d, (0, hp - heads))
    seg = seg_ids.reshape(1, tokens)
    alog, skip = a_log.reshape(1, hp), skip_d.reshape(1, hp)
    state_outs = [((tokens, wc), bf16), ((2 * SPAN * (nb - 1), wc), bf16), ((16, wc), f32)]
    dma = pltpu.SemaphoreType.DMA
    first = call(
        functools.partial(first_kernel, heads, hp, nch),
        [ANY, ANY, ANY] + [VMEM] * 5,
        [((STATE + TAIL, wc), bf16)] + state_outs
        + [
            ((tokens, 2 * STATE), bf16),
            ((STATE, tokens), bf16),
            ((5 * hp, tokens), f32),
            ((hp, 128), f32),
            ((3 * tokens, 2 * SPAN), bf16),
            ((TAIL, width), bf16),
            ((TAIL, 2 * STATE), bf16),
            ((KERNEL, 2 * STATE), f32),
        ],
        [
            pltpu.VMEM((tokens, wc), bf16),
            pltpu.VMEM((tokens, 2 * STATE), bf16),
            pltpu.VMEM((TAIL, width), bf16),
            dma((7,)),
        ],
        name="first",
    )
    msg, xc, ls, kr, bcc, bt, rows, kcols, shift, xhead, bchead, taps_bc = first(
        x_in, bc_in, conv_bc, conv_x, dt, alog, skip, seg
    )
    xcs, lss, krs, msgs = [xc], [ls], [kr], [msg]
    recv1 = [lax.ppermute(msg, "seq", ring)]
    if nch == 2:
        msg, xc, ls, kr = call(
            functools.partial(next_kernel, hp, per_chunk),
            [ANY] + [VMEM] * 5,
            [((STATE, wc), bf16)] + state_outs,
            [pltpu.VMEM((tokens, wc), bf16), dma],
            name="next",
        )(x_in, conv_x, shift, bt, rows, kcols)
        xcs.append(xc)
        lss.append(ls)
        krs.append(kr)
        recv1.append(lax.ppermute(msg, "seq", ring))
    relay, xw8, x8, b8, c8, flag = call(
        functools.partial(relay_first, nch),
        [VMEM] * (7 + nch),
        [
            ((STATE, wc), bf16),
            ((TAIL, width), bf16),
            ((8, width), f32),
            ((TAIL, STATE), bf16),
            ((TAIL, STATE), bf16),
            ((8, 128), f32),
        ],
        name="relay_first",
    )(recv1[0], xhead, bchead, conv_x, taps_bc, seg, bcc, *krs)
    recvs = [[recv1[c]] for c in range(nch)]
    relays = [relay]
    if rounds > 1:
        recvs[0].append(lax.ppermute(relay, "seq", ring))
    if nch == 2:
        (relay,) = call(relay_next, [VMEM] * 5, [((STATE, wc), bf16)], name="relay_next")(
            recv1[1], krs[1], b8, xw8, flag
        )
        relays.append(relay)
        if rounds > 1:
            recvs[1].append(lax.ppermute(relay, "seq", ring))
    for _ in range(2, rounds):
        for c in range(nch):
            again = recvs[c][-1].astype(f32) * (krs[c][0:1] * flag[0:1, 0:1])
            recvs[c].append(lax.ppermute(again.astype(bf16), "seq", ring))
    local = []
    for c in range(nch):
        local.append(
            call(
                functools.partial(local_kernel, hp, c * per_chunk),
                [ANY] + [VMEM] * 7 + [ANY],
                [((tokens, wc), f32), ((tokens, wc), f32), ((8, wc), f32)],
                [pltpu.VMEM((tokens, wc), bf16), dma],
                name=f"local{c}",
            )(z_in, xcs[c], lss[c], krs[c], bcc, bt, rows, seg, msgs[0] if c == 0 else relays[-1])
        )
    (cg,) = call(rank_kernel, [VMEM] * 3, [((tokens, 3 * STATE), bf16)], name="rank")(bcc, b8, c8)
    sums = jnp.zeros((1, tokens), f32)
    gated = []
    for c in range(nch):
        n = len(recvs[c])
        g, sums = call(
            functools.partial(gate_kernel, n, c),
            [VMEM] * (8 + n),
            [((tokens, wc), f32), ((1, tokens), f32)],
            name=f"gate{c}",
        )(cg, xw8, x8, flag, *local[c], sums, *recvs[c])
        gated.append(g)
    gathered = lax.all_gather(sums, "head", axis=0, tiled=True)
    out = pl.pallas_call(
        functools.partial(norm_kernel, nch),
        grid=(nb,),
        out_shape=jax.ShapeDtypeStruct((tokens, width), bf16),
        in_specs=[
            pl.BlockSpec((gathered.shape[0], SPAN), lambda i: (0, i)),
            pl.BlockSpec((1, width), lambda i: (0, 0)),
        ]
        + [VMEM] * nch,
        out_specs=pl.BlockSpec((SPAN, width), lambda i: (i, 0)),
        compiler_params=pltpu.CompilerParams(vmem_limit_bytes=24 << 20),
        name="norm",
    )(gathered, norm_gain.reshape(1, width), *gated)
    return out


def solution(mesh):
    in_specs = (
        P("seq", "head"),
        P("seq", "head"),
        P("seq", None),
        P(None, "head"),
        P(),
        P("head", "seq"),
        P("head"),
        P("head"),
        P("head"),
        P("seq"),
    )
    return jax.shard_map(
        per_device, mesh=mesh, in_specs=in_specs, out_specs=P("seq", "head"), check_vma=False
    )
```

```python
import functools
import jax
import jax.numpy as jnp
from jax import lax
from jax.experimental import pallas as pl
from jax.experimental.pallas import tpu as pltpu
from jax.sharding import PartitionSpec as P

HEADS = 128
HEAD_DIM = 64
STATE = 128
GROUPS = 8
KERNEL = 4
SPAN = 128
LOG2E = 1.4426950408889634
TINY = 1e-37
TAIL = 16
TILE = 512
f32 = jnp.float32
bf16 = jnp.bfloat16


def mm(a, b, ca=1, cb=0):
    return lax.dot_general(a, b, (((ca,), (cb,)), ((), ())), preferred_element_type=f32)


def iota(shape, axis):
    return lax.broadcasted_iota(jnp.int32, shape, axis)


def split(value, parts):
    pieces = []
    for _ in range(parts):
        piece = value.astype(bf16)
        pieces.append(piece)
        value = value - piece.astype(f32)
    return jnp.concatenate(pieces, 0)


def expander(heads, parts, width, first):
    row = iota((parts * heads, width), 0) & (heads - 1)
    col = (iota((parts * heads, width), 1) >> 6) + first
    return jnp.where(row == col, 1.0, 0.0).astype(bf16)


def silu_from_half(half):
    return half + half * jnp.tanh(half)


def blk(b):
    return slice(b * SPAN, (b + 1) * SPAN)


def to_column(row):
    n = row.shape[1]
    rows = jnp.where(iota((16, n), 0) == 0, row, 0.0).astype(bf16)
    return mm(rows, jnp.ones((16, 128), bf16), 0, 0)


def chunk_state(hp, first, x, taps, shift, bt, rows, kcols, drop, xc, lstate, krows, msg):
    tokens, wc = x.shape
    nb = tokens // SPAN
    kr = mm(split(kcols, 3), expander(hp, 3, wc, first), 0, 0)[:16]
    krows[...] = kr
    tile = min(TILE, wc)
    ex = expander(hp, 2, wc, first)
    for j in range(wc // tile):
        js = slice(j * tile, (j + 1) * tile)
        state = None
        for b in range(nb):
            if b == 0:
                sh = mm(shift[0 : 3 * SPAN, SPAN:], x[blk(0), js])
            else:
                sh = mm(
                    shift[3 * SPAN * b : 3 * SPAN * (b + 1), :],
                    x[(b - 1) * SPAN : (b + 1) * SPAN, js],
                )
            half = sh[0:SPAN] * taps[0:1, js] + sh[SPAN : 2 * SPAN] * taps[1:2, js]
            half = half + sh[2 * SPAN :] * taps[2:3, js]
            half = half + x[blk(b), js].astype(f32) * taps[3:4, js]
            act = silu_from_half(half)
            if b == 0:
                top = act[0:TAIL]
                top = jnp.where(iota(top.shape, 0).astype(f32) < drop, 0.0, top)
                act = jnp.concatenate([top, act[TAIL:]], 0)
            act = act.astype(bf16)
            xc[blk(b), js] = act
            to_end = mm(split(rows[3 * hp : 4 * hp, blk(b)], 2), ex[:, js], 0, 0)
            weighted = (act.astype(f32) * to_end).astype(bf16)
            fresh = mm(bt[:, blk(b)], weighted)
            state = fresh if b == 0 else state * kr[b : b + 1, js] + fresh
            if b < nb - 1:
                lstate[blk(b), js] = state.astype(bf16)
        msg[0:STATE, js] = state.astype(bf16)


def first_kernel(
    heads, hp, nch,
    x_any, bc_any, tapbc_any, tapx_any, dt_any, alog_any, skip_any, seg_any,
    msg, xc, lstate, krows, bcc, bt, rows, kcols, shift, xhead, bchead, taps_bc, tapx, seg_ref,
    *refs,
):
    xnext = refs[: nch - 1]
    xbuf, bcbuf, xtail, dt_ref, alog_ref, skip_ref, sems = refs[nch - 1 :]
    tokens, wc = xbuf.shape
    nb = tokens // SPAN
    group = lax.axis_index("head") * heads // (HEADS // GROUPS)
    col_b = pl.multiple_of(group * STATE, STATE)
    col_c = pl.multiple_of((group + GROUPS) * STATE, STATE)
    width = nch * wc
    small = [(dt_any, dt_ref), (alog_any, alog_ref), (skip_any, skip_ref), (seg_any, seg_ref), (tapx_any, tapx)]
    small = [pltpu.make_async_copy(a, b, sems.at[7 + i]) for i, (a, b) in enumerate(small)]
    copies = [
        pltpu.make_async_copy(bc_any.at[:, pl.ds(col_b, STATE)], bcbuf.at[:, 0:STATE], sems.at[0]),
        pltpu.make_async_copy(bc_any.at[:, pl.ds(col_c, STATE)], bcbuf.at[:, STATE:], sems.at[1]),
        pltpu.make_async_copy(tapbc_any.at[:, pl.ds(col_b, STATE)], taps_bc.at[:, 0:STATE], sems.at[2]),
        pltpu.make_async_copy(tapbc_any.at[:, pl.ds(col_c, STATE)], taps_bc.at[:, STATE:], sems.at[3]),
        pltpu.make_async_copy(x_any.at[:, 0:wc], xbuf, sems.at[4]),
        pltpu.make_async_copy(x_any.at[tokens - TAIL :, :], xtail, sems.at[5]),
        pltpu.make_async_copy(x_any.at[0:TAIL, :], xhead, sems.at[6]),
    ]
    if nch == 2:
        copies.append(pltpu.make_async_copy(x_any.at[:, wc:], xnext[0], sems.at[12]))
    for copy in small + copies:
        copy.start()
    for copy in small:
        copy.wait()
    seg = seg_ref[...].astype(f32)
    seg_first = seg[:, 0:1]
    seg_last = [seg[:, (b + 1) * SPAN - 1 : (b + 1) * SPAN] for b in range(nb)]
    eye = iota((hp, hp), 0) == iota((hp, hp), 1)
    rate = jnp.exp(jnp.sum(jnp.where(eye, alog_ref[...], 0.0), axis=1, keepdims=True))
    skip = jnp.sum(jnp.where(eye, skip_ref[...], 0.0), axis=1, keepdims=True)
    dt = dt_ref[...]
    parts = split(dt * (rate * -LOG2E), 3)
    tri = jnp.where(iota((SPAN, SPAN), 0) <= iota((SPAN, SPAN), 1), 1.0, 0.0).astype(bf16)
    sums = mm(jnp.concatenate([parts[:, blk(b)] for b in range(nb)], 0), tri)
    lane = iota((hp, SPAN), 1)
    lane1 = iota((1, SPAN), 1)
    before = jnp.zeros((hp, 1), f32)
    kc = jnp.where(lane == 11, skip, 0.0)
    for b in range(nb):
        three = sums[3 * hp * b : 3 * hp * (b + 1)]
        cum = three[0:hp] + three[hp : 2 * hp] + three[2 * hp :]
        last = cum[:, SPAN - 1 : SPAN]
        segb, dtb = seg[:, blk(b)], dt[:, blk(b)]
        total = cum + before
        rows[0:hp, blk(b)] = cum
        rows[hp : 2 * hp, blk(b)] = jnp.exp2(total) * jnp.where(segb == seg_first, 1.0, 0.0)
        if b > 0:
            rows[2 * hp : 3 * hp, blk(b)] = jnp.exp2(cum) * jnp.where(segb == seg_last[b - 1], 1.0, 0.0)
            keep = jnp.exp2(last) * jnp.where(seg_last[b] == seg_last[b - 1], 1.0, 0.0)
            kc = kc + jnp.where(lane == b, keep, 0.0)
        else:
            rows[2 * hp : 3 * hp, blk(b)] = jnp.zeros((hp, SPAN), f32)
            is_drop = jnp.where((lane1 < KERNEL - 1) & (segb == seg_first), 1.0, 0.0)
            drop = jnp.sum(is_drop, axis=1, keepdims=True)
            early = jnp.exp2(jnp.where(lane < KERNEL - 1, -cum, 0.0)) * dtb * is_drop
            kc = kc + pltpu.roll(early, 8, 1)
        rows[3 * hp : 4 * hp, blk(b)] = jnp.exp2(last - cum) * dtb * jnp.where(segb == seg_last[b], 1.0, 0.0)
        rows[4 * hp : 5 * hp, blk(b)] = cum - jnp.log2(jnp.maximum(dtb, TINY))
        before = before + last
    fend = jnp.exp2(before) * jnp.where(seg_last[-1] == seg_first, 1.0, 0.0)
    kc = kc + jnp.where(lane == 0, fend, 0.0) + jnp.where(lane == 16, drop, 0.0)
    kcols[...] = kc
    delta = iota((SPAN, SPAN), 1) - iota((SPAN, SPAN), 0)
    for b in range(nb):
        segcol = to_column(seg[:, blk(b)])
        same = segcol == seg[:, blk(b)]
        for k in range(KERNEL - 1):
            back = KERNEL - 1 - k
            r = slice(3 * SPAN * b + SPAN * k, 3 * SPAN * b + SPAN * (k + 1))
            shift[r, SPAN:] = jnp.where((delta == -back) & same, 1.0, 0.0).astype(bf16)
            if b > 0:
                same_prev = segcol == seg[:, blk(b - 1)]
                shift[r, 0:SPAN] = jnp.where((delta == SPAN - back) & same_prev, 1.0, 0.0).astype(bf16)
            else:
                shift[r, 0:SPAN] = jnp.zeros((SPAN, SPAN), bf16)
    for copy in copies[:4]:
        copy.wait()
    bchead[...] = bcbuf[0:TAIL, :]
    tb = taps_bc[...] * 0.5
    for b in range(nb):
        if b == 0:
            sh = mm(shift[0 : 3 * SPAN, SPAN:], bcbuf[blk(0), :])
        else:
            sh = mm(shift[3 * SPAN * b : 3 * SPAN * (b + 1), :], bcbuf[(b - 1) * SPAN : (b + 1) * SPAN, :])
        half = sh[0:SPAN] * tb[0:1] + sh[SPAN : 2 * SPAN] * tb[1:2]
        half = half + sh[2 * SPAN :] * tb[2:3] + bcbuf[blk(b), :].astype(f32) * tb[3:4]
        act = silu_from_half(half).astype(bf16)
        bcc[blk(b), :] = act
        bt[:, blk(b)] = act[:, 0:STATE].T
    copies[4].wait()
    chunk_state(
        hp, 0, xbuf, tapx[:, 0:wc] * 0.5, shift, bt, rows, kc, drop, xc, lstate, krows, msg
    )
    for copy in copies[5:]:
        copy.wait()
    lane_last = iota((1, SPAN), 1)
    is_tail = jnp.where((lane_last >= SPAN - (KERNEL - 1)) & (seg[:, blk(nb - 1)] == seg_last[-1]), 1.0, 0.0)
    first_valid = 8.0 - jnp.sum(is_tail, axis=1, keepdims=True)

    def tail_of(value):
        rows8 = value.astype(f32)[8:16]
        return jnp.where(iota(rows8.shape, 0).astype(f32) >= first_valid, rows8, 0.0)

    tile0 = tail_of(xtail[:, 0:wc])
    if nch == 2:
        tile0 = tile0 + pltpu.roll(tail_of(xtail[:, wc:]), 4, 0)
    tile0 = jnp.where(iota(tile0.shape, 0) == 0, seg_last[-1] + 1.0, tile0)
    tail_bc = tail_of(bcbuf[tokens - TAIL :, :])
    tile1 = tail_bc[:, 0:STATE] + pltpu.roll(tail_bc[:, STATE:], 4, 0)
    if wc > STATE:
        tile1 = jnp.concatenate([tile1, jnp.zeros((8, wc - STATE), f32)], 1)
    msg[STATE:, :] = jnp.concatenate([tile0, tile1], 0).astype(bf16)


def next_kernel(hp, first, xbuf, tapx, shift, bt, rows, kcols, msg, xc, lstate, krows):
    wc = xbuf.shape[1]
    chunk_state(
        hp, first, xbuf, tapx[:, wc : 2 * wc] * 0.5, shift, bt, rows, kcols[...],
        kcols[0:1, 16:17], xc, lstate, krows, msg,
    )


def early_conv(halo, head, taps):
    rows = jnp.concatenate([halo, head.astype(f32)[0:8]], 0)
    half = rows[5:13] * taps[0:1]
    for k in range(1, KERNEL):
        half = half + rows[5 + k : 13 + k] * taps[k : k + 1]
    return silu_from_half(half)


def relay_state(krows, recv, b8, xw8, flag):
    base = recv.astype(f32) * flag + mm(b8, xw8, 0, 0)
    return (base * krows[0:1]).astype(bf16)


def relay_first(nch, recv, xhead, bchead, tapx, taps_bc, seg_ref, bcc, *refs):
    krows = refs[:nch]
    out, xw8_ref, x8_ref, b8_ref, c8_ref, flag_ref = refs[nch:]
    wc = out.shape[1]
    tile = recv[STATE:, :].astype(f32)
    tile0, tile1 = tile[0:8], tile[8:16, 0:STATE]
    seg = seg_ref[:, 0:SPAN].astype(f32)
    seg_first = seg[:, 0:1]
    lane = iota((1, SPAN), 1)
    drop = jnp.sum(
        jnp.where((lane < KERNEL - 1) & (seg == seg_first), 1.0, 0.0), axis=1, keepdims=True
    )
    joined = jnp.where(tile0[0:1, 0:1] == seg_first + 1.0, 1.0, 0.0)
    flag = joined * jnp.where(lax.axis_index("seq") == 0, 0.0, 1.0)
    flag_ref[...] = jnp.broadcast_to(flag, (8, 128))

    def lower(value):
        return jnp.where(iota(value.shape, 0) >= 8 - (KERNEL - 1), value, 0.0) * flag

    def early(value):
        return jnp.where(iota(value.shape, 0).astype(f32) < drop, value, 0.0)

    zero8 = lambda n: jnp.zeros((8, n), f32)
    halo = [lower(tile0)]
    if nch == 2:
        halo.append(lower(pltpu.roll(tile0, 4, 0)))
    bc8 = early_conv(
        jnp.concatenate([lower(tile1), lower(pltpu.roll(tile1, 4, 0))], 1), bchead[...], taps_bc[...] * 0.5
    )
    b8 = jnp.concatenate([early(bc8[:, 0:STATE]), zero8(STATE)], 0).astype(bf16)
    b8_ref[...] = b8
    old = bcc[0:TAIL, STATE:].astype(f32)
    c8 = jnp.where(iota((8, STATE), 0).astype(f32) < drop, bc8[:, STATE:], old[0:8])
    c8_ref[...] = jnp.concatenate([c8, old[8:16]], 0).astype(bf16)
    for c in range(nch):
        cs = slice(c * wc, (c + 1) * wc)
        x8 = early(early_conv(halo[c], xhead[:, cs], tapx[:, cs] * 0.5)).astype(bf16).astype(f32)
        kr = krows[c][...]
        x8_ref[:, cs] = x8 * kr[11:12]
        xw8 = jnp.concatenate([x8 * kr[8:16], zero8(wc)], 0).astype(bf16)
        xw8_ref[:, cs] = xw8
        if c == 0:
            out[...] = relay_state(kr, recv[0:STATE, :], b8, xw8, flag)


def relay_next(recv, krows, b8, xw8, flag, order, out):
    wc = out.shape[1]
    out[...] = relay_state(krows[...], recv[...], b8[...], xw8[:, wc:], flag[0:1, 0:1])


def local_kernel(
    hp, first, z_any, xc, lstate, krows, bcc, bt, rows, seg_ref, cg, recv, xw8, x8, flag, order,
    a_ref, q_ref, zbuf, sem,
):
    tokens, wc = zbuf.shape
    nb = tokens // SPAN
    lane0 = first * HEAD_DIM
    lanes = slice(lane0, lane0 + wc)
    copy = pltpu.make_async_copy(z_any.at[:, lanes], zbuf, sem)
    copy.start()
    seg = seg_ref[...].astype(f32)
    ex = expander(hp, 2, wc, first)
    head_of = iota((128, SPAN), 0) & (hp - 1)
    low = iota((SPAN, 128), 1) < HEAD_DIM
    tri = iota((SPAN, SPAN), 0) >= iota((SPAN, SPAN), 1)
    entering = jnp.concatenate(
        [
            (recv[0:STATE, :].astype(f32) * flag[0:1, 0:1]).astype(bf16),
            xw8[:, lanes],
            jnp.zeros((128 - TAIL, wc), bf16),
        ],
        0,
    )
    for b in range(nb):
        segcol = to_column(seg[:, blk(b)])
        mask = (segcol == seg[:, blk(b)]) & tri
        c_blk = bcc[blk(b), STATE:]
        scores = jnp.where(mask, mm(c_blk, bt[:, blk(b)]), 0.0)
        scores = jnp.concatenate([scores, scores], 1)
        cum = split(rows[0:hp, blk(b)], 3)
        neg_q = split(-rows[4 * hp : 5 * hp, blk(b)], 3)
        ones = jnp.ones((3 * hp, SPAN), bf16)
        pad = jnp.zeros((128 - 6 * hp, SPAN), bf16)
        left = jnp.concatenate([cum, ones, pad], 0).T
        right = jnp.concatenate([ones, neg_q, pad], 0).astype(f32)
        f_exp = mm(split(rows[hp : 2 * hp, blk(b)], 2), ex, 0, 0)
        inflow = mm(cg[blk(b), :], entering)
        if b > 0:
            e_exp = mm(split(rows[2 * hp : 3 * hp, blk(b)], 2), ex, 0, 0)
            carry = mm(c_blk, lstate[blk(b - 1), :])
        if b == 0:
            copy.wait()
        for j in range(wc // 128):
            js = slice(j * 128, (j + 1) * 128)
            xj = xc[blk(b), js]
            h = first + 2 * j
            sel = [jnp.where(head_of == h + i, right, 0.0).astype(bf16) for i in range(2)]
            decay = jnp.exp2(jnp.minimum(mm(left, jnp.concatenate(sel, 1)), 8.0))
            zero = jnp.zeros_like(xj)
            pair = jnp.concatenate([jnp.where(low, xj, zero), jnp.where(low, zero, xj)], 0)
            y = mm((scores * decay).astype(bf16), pair) + xj.astype(f32) * krows[11:12, js]
            if b > 0:
                y = y + e_exp[:, js] * carry[:, js]
            else:
                top = y[0:8] + x8[:, lane0 + j * 128 : lane0 + (j + 1) * 128]
                y = jnp.concatenate([top, y[8:]], 0)
            f = f_exp[:, js]
            sz = silu_from_half(zbuf[blk(b), js].astype(f32) * 0.5)
            a_ref[blk(b), js] = (y + f * inflow[:, js]) * sz
            q_ref[blk(b), js] = f * sz


def rank_kernel(bcc, b8, c8, cg):
    tokens = bcc.shape[0]
    b_pad = jnp.concatenate([b8[...], jnp.zeros((128 - TAIL, STATE), bf16)], 0)
    cg[:, 0:STATE] = bcc[:, STATE:]
    cg[0:TAIL, 0:STATE] = c8[...]
    g = mm(cg[:, 0:STATE], b_pad, 1, 1)
    causal = iota((tokens, 128), 0) >= iota((tokens, 128), 1)
    cg[:, STATE:] = jnp.where(causal, g, 0.0).astype(bf16)


def gate_kernel(nrecv, cg, flag, a_ref, q_ref, prev, *refs):
    recvs, (gated, sums) = refs[:nrecv], refs[nrecv:]
    tokens, wc = a_ref.shape
    if nrecv == 1:
        total = recvs[0][...]
    elif nrecv > 1:
        total = recvs[0][...].astype(f32)
        for r in recvs[1:]:
            total = total + r[...].astype(f32)
        total = total.astype(bf16)
    tile = min(256, wc)
    for b in range(tokens // SPAN):
        acc = None
        for j in range(wc // tile):
            js = slice(j * tile, (j + 1) * tile)
            g = a_ref[blk(b), js]
            if nrecv:
                g = g + (q_ref[blk(b), js] * flag[0:1, 0:1]) * mm(cg[blk(b), 0:STATE], total[:, js])
            gated[blk(b), js] = g
            sq = g * g
            for i in range(tile // 128):
                part = sq[:, i * 128 : (i + 1) * 128]
                acc = part if acc is None else acc + part
        sums[:, blk(b)] = prev[:, blk(b)] + jnp.sum(acc.T, axis=0, keepdims=True)


def norm_kernel(nch, sums, gain, *refs):
    gated, (out, buf, sems) = refs[:nch], refs[nch:]
    tokens, wc = gated[0].shape
    scale = lax.rsqrt(sums[...] / (HEADS * HEAD_DIM) + 1e-05)
    ones = jnp.ones((48, 128), bf16)
    copies = []
    for b in range(tokens // SPAN):
        wide = jnp.where(iota((16, SPAN), 0) == 0, scale[:, blk(b)], 0.0)
        col = mm(split(wide, 3), ones, 0, 0)
        for c in range(nch):
            for j in range(wc // 128):
                js = slice(j * 128, (j + 1) * 128)
                at = slice(c * wc + j * 128, c * wc + (j + 1) * 128)
                buf[blk(b), at] = (gated[c][blk(b), js] * col * gain[:, at]).astype(bf16)
        copy = pltpu.make_async_copy(buf.at[blk(b), :], out.at[blk(b), :], sems.at[b])
        copy.start()
        copies.append(copy)
    for copy in copies:
        copy.wait()


VMEM = pl.BlockSpec(memory_space=pltpu.VMEM)
ANY = pl.BlockSpec(memory_space=pl.ANY)


def call(body, ins, outs, scratch=(), name=None, limit=24 << 20):
    return pl.pallas_call(
        body,
        out_shape=[pltpu.VMEM(shape, dtype) for shape, dtype in outs],
        in_specs=ins,
        out_specs=[VMEM] * len(outs),
        scratch_shapes=list(scratch),
        compiler_params=pltpu.CompilerParams(vmem_limit_bytes=limit),
        name=name,
    )


def per_device(x_in, z_in, bc_in, conv_x, conv_bc, dt, a_log, skip_d, norm_gain, seg_ids):
    tokens, width = x_in.shape
    heads = dt.shape[0]
    nb = tokens // SPAN
    hp = max(16, heads)
    peers = lax.axis_size("seq")
    rounds = max(1, peers // 2)
    nch = 2 if width % 512 == 0 else 1
    wc = width // nch
    per_chunk = heads // nch
    ring = [(i, (i + 1) % peers) for i in range(peers)]
    if hp != heads:
        dt = jnp.pad(dt, ((0, hp - heads), (0, 0)))
        a_log = jnp.pad(a_log, (0, hp - heads))
        skip_d = jnp.pad(skip_d, (0, hp - heads))
    seg = seg_ids.reshape(1, tokens)
    alog, skip = a_log.reshape(1, hp), skip_d.reshape(1, hp)
    state_outs = [((tokens, wc), bf16), ((SPAN * (nb - 1), wc), bf16), ((16, wc), f32)]
    dma = pltpu.SemaphoreType.DMA
    hbm = lambda value: pltpu.with_memory_space_constraint(value, pltpu.HBM)
    first = call(
        functools.partial(first_kernel, heads, hp, nch),
        [ANY] * 8,
        [((STATE + TAIL, wc), bf16)] + state_outs
        + [
            ((tokens, 2 * STATE), bf16),
            ((STATE, tokens), bf16),
            ((5 * hp, tokens), f32),
            ((hp, 128), f32),
            ((3 * tokens, 2 * SPAN), bf16),
            ((TAIL, width), bf16),
            ((TAIL, 2 * STATE), bf16),
            ((KERNEL, 2 * STATE), f32),
            ((KERNEL, width), f32),
            ((1, tokens), jnp.int32),
        ]
        + [((tokens, wc), bf16)] * (nch - 1),
        [
            pltpu.VMEM((tokens, wc), bf16),
            pltpu.VMEM((tokens, 2 * STATE), bf16),
            pltpu.VMEM((TAIL, width), bf16),
            pltpu.VMEM((hp, tokens), f32),
            pltpu.VMEM((1, hp), f32),
            pltpu.VMEM((1, hp), f32),
            dma((13,)),
        ],
        name="first",
    )
    (
        msg, xc, ls, kr, bcc, bt, rows, kcols, shift, xhead, bchead, taps_bc, tapx, seg, *xnext
    ) = first(*[hbm(v) for v in (x_in, bc_in, conv_bc, conv_x, dt, alog, skip, seg)])
    xcs, lss, krs = [xc], [ls], [kr]
    recv1 = [lax.ppermute(msg, "seq", ring)]
    if nch == 2:
        msg, xc, ls, kr = call(
            functools.partial(next_kernel, hp, per_chunk),
            [VMEM] * 6,
            [((STATE, wc), bf16)] + state_outs,
            name="next",
        )(xnext[0], tapx, shift, bt, rows, kcols)
        xcs.append(xc)
        lss.append(ls)
        krs.append(kr)
        recv1.append(lax.ppermute(msg, "seq", ring))
    relay, xw8, x8, b8, c8, flag = call(
        functools.partial(relay_first, nch),
        [VMEM] * (7 + nch),
        [
            ((STATE, wc), bf16),
            ((TAIL, width), bf16),
            ((8, width), f32),
            ((TAIL, STATE), bf16),
            ((TAIL, STATE), bf16),
            ((8, 128), f32),
        ],
        name="relay_first",
    )(recv1[0], xhead, bchead, tapx, taps_bc, seg, bcc, *krs)
    later = [[] for c in range(nch)]
    if rounds > 1:
        later[0].append(lax.ppermute(relay, "seq", ring))
    (cg,) = call(rank_kernel, [VMEM] * 3, [((tokens, 2 * STATE), bf16)], name="rank")(bcc, b8, c8)
    local = []
    for c in range(nch):
        if c == 1:
            (relay,) = call(relay_next, [VMEM] * 5 + [ANY], [((STATE, wc), bf16)], name="relay_next")(
                recv1[1], krs[1], b8, xw8, flag, local[0][1]
            )
            if rounds > 1:
                later[1].append(lax.ppermute(relay, "seq", ring))
        local.append(
            call(
                functools.partial(local_kernel, hp, c * per_chunk),
                [ANY] + [VMEM] * 12 + [ANY],
                [((tokens, wc), f32), ((tokens, wc), f32)],
                [pltpu.VMEM((tokens, wc), bf16), dma],
                name=f"local{c}",
            )(z_in, xcs[c], lss[c], krs[c], bcc, bt, rows, seg, cg, recv1[c], xw8, x8, flag, relay)
        )
    for _ in range(2, rounds):
        for c in range(nch):
            again = later[c][-1].astype(f32) * (krs[c][0:1] * flag[0:1, 0:1])
            later[c].append(lax.ppermute(again.astype(bf16), "seq", ring))
    sums = jnp.zeros((1, tokens), f32)
    gated = []
    for c in range(nch):
        n = len(later[c])
        g, sums = call(
            functools.partial(gate_kernel, n),
            [VMEM] * (5 + n),
            [((tokens, wc), f32), ((1, tokens), f32)],
            name=f"gate{c}",
        )(cg, flag, *local[c], sums, *later[c])
        gated.append(g)
    members = lax.axis_size("head")
    step = 1
    while step < members:
        sums = sums + lax.ppermute(sums, "head", [(i, i ^ step) for i in range(members)])
        step *= 2
    return pl.pallas_call(
        functools.partial(norm_kernel, nch),
        out_shape=jax.ShapeDtypeStruct((tokens, width), bf16),
        in_specs=[VMEM] * (2 + nch),
        out_specs=ANY,
        scratch_shapes=[pltpu.VMEM((tokens, width), bf16), dma((nb,))],
        compiler_params=pltpu.CompilerParams(vmem_limit_bytes=24 << 20),
        name="norm",
    )(sums, norm_gain.reshape(1, width), *gated)


def solution(mesh):
    in_specs = (
        P("seq", "head"),
        P("seq", "head"),
        P("seq", None),
        P(None, "head"),
        P(),
        P("head", "seq"),
        P("head"),
        P("head"),
        P("head"),
        P("seq"),
    )
    return jax.shard_map(
        per_device, mesh=mesh, in_specs=in_specs, out_specs=P("seq", "head"), check_vma=False
    )
```

```python
import functools
import jax
import jax.numpy as jnp
from jax import lax
from jax.experimental import pallas as pl
from jax.experimental.pallas import tpu as pltpu
from jax.sharding import PartitionSpec as P

HEADS = 128
HEAD_DIM = 64
STATE = 128
GROUPS = 8
KERNEL = 4
SPAN = 128
LOG2E = 1.4426950408889634
TINY = 1e-37
TAIL = 16
TILE = 512
f32 = jnp.float32
bf16 = jnp.bfloat16


def mm(a, b, ca=1, cb=0):
    return lax.dot_general(a, b, (((ca,), (cb,)), ((), ())), preferred_element_type=f32)


def iota(shape, axis):
    return lax.broadcasted_iota(jnp.int32, shape, axis)


def split(value, parts):
    pieces = []
    for _ in range(parts):
        piece = value.astype(bf16)
        pieces.append(piece)
        value = value - piece.astype(f32)
    return jnp.concatenate(pieces, 0)


def expander(heads, parts, width, first):
    row = iota((parts * heads, width), 0) & (heads - 1)
    col = (iota((parts * heads, width), 1) >> 6) + first
    return jnp.where(row == col, 1.0, 0.0).astype(bf16)


def reached(hops):
    return jnp.where(lax.axis_index("seq") >= hops, 1.0, 0.0)


def onward(peers, members, start):
    moves = []
    for i in range(peers):
        for h in range(members):
            ahead = (i + 1 if i + 1 < peers else start) * members + h
            moves.append((i * members + h, ahead if i >= start else i * members + (h ^ 1)))
    return moves


def silu_from_half(half):
    return half + half * jnp.tanh(half)


def blk(b):
    return slice(b * SPAN, (b + 1) * SPAN)


def to_column(row):
    n = row.shape[1]
    rows = jnp.where(iota((16, n), 0) == 0, row, 0.0).astype(bf16)
    return mm(rows, jnp.ones((16, 128), bf16), 0, 0)


def chunk_state(hp, first, x, taps, shift, bt, rows, kcols, drop, xc, lstate, krows, msg):
    tokens, wc = x.shape
    nb = tokens // SPAN
    kr = mm(split(kcols, 3), expander(hp, 3, wc, first), 0, 0)[:16]
    krows[...] = kr
    tile = min(TILE, wc)
    ex = expander(hp, 2, wc, first)
    steps = [(j, b) for j in range(wc // tile) for b in range(nb)]

    def gather(j, b):
        js = slice(j * tile, (j + 1) * tile)
        if b == 0:
            return mm(shift[0 : 3 * SPAN, SPAN:], x[blk(0), js])
        return mm(shift[3 * SPAN * b : 3 * SPAN * (b + 1), :], x[(b - 1) * SPAN : (b + 1) * SPAN, js])

    to_end = [mm(split(rows[3 * hp : 4 * hp, blk(b)], 2), ex, 0, 0) for b in range(nb)]
    ready = gather(*steps[0])
    state = None
    for i, (j, b) in enumerate(steps):
        js = slice(j * tile, (j + 1) * tile)
        sh = ready
        if i + 1 < len(steps):
            ready = gather(*steps[i + 1])
        half = sh[0:SPAN] * taps[0:1, js] + sh[SPAN : 2 * SPAN] * taps[1:2, js]
        half = half + sh[2 * SPAN :] * taps[2:3, js]
        half = half + x[blk(b), js].astype(f32) * taps[3:4, js]
        act = silu_from_half(half)
        if b == 0:
            top = act[0:TAIL]
            top = jnp.where(iota(top.shape, 0).astype(f32) < drop, 0.0, top)
            act = jnp.concatenate([top, act[TAIL:]], 0)
        act = act.astype(bf16)
        xc[blk(b), js] = act
        weighted = (act.astype(f32) * to_end[b][:, js]).astype(bf16)
        fresh = mm(bt[:, blk(b)], weighted)
        state = fresh if b == 0 else state * kr[b : b + 1, js] + fresh
        if b < nb - 1:
            lstate[blk(b), js] = state.astype(bf16)
        else:
            msg[0:STATE, js] = state.astype(bf16)


def first_kernel(
    heads, hp, nch,
    x_any, bc_any, tapbc_any, tapx_any, dt_any, alog_any, skip_any, seg_any,
    msg, xc, lstate, krows, bcc, bt, rows, kcols, shift, xhead, bchead, taps_bc, tapx, seg_ref,
    *refs,
):
    xnext = refs[: nch - 1]
    xbuf, bcbuf, xtail, dt_ref, alog_ref, skip_ref, sems = refs[nch - 1 :]
    tokens, wc = xbuf.shape
    nb = tokens // SPAN
    group = lax.axis_index("head") * heads // (HEADS // GROUPS)
    col_b = pl.multiple_of(group * STATE, STATE)
    col_c = pl.multiple_of((group + GROUPS) * STATE, STATE)
    width = nch * wc
    small = [(dt_any, dt_ref), (alog_any, alog_ref), (skip_any, skip_ref), (seg_any, seg_ref), (tapx_any, tapx)]
    small = [pltpu.make_async_copy(a, b, sems.at[7 + i]) for i, (a, b) in enumerate(small)]
    copies = [
        pltpu.make_async_copy(bc_any.at[:, pl.ds(col_b, STATE)], bcbuf.at[:, 0:STATE], sems.at[0]),
        pltpu.make_async_copy(bc_any.at[:, pl.ds(col_c, STATE)], bcbuf.at[:, STATE:], sems.at[1]),
        pltpu.make_async_copy(tapbc_any.at[:, pl.ds(col_b, STATE)], taps_bc.at[:, 0:STATE], sems.at[2]),
        pltpu.make_async_copy(tapbc_any.at[:, pl.ds(col_c, STATE)], taps_bc.at[:, STATE:], sems.at[3]),
        pltpu.make_async_copy(x_any.at[:, 0:wc], xbuf, sems.at[4]),
        pltpu.make_async_copy(x_any.at[tokens - TAIL :, :], xtail, sems.at[5]),
        pltpu.make_async_copy(x_any.at[0:TAIL, :], xhead, sems.at[6]),
    ]
    if nch == 2:
        copies.append(pltpu.make_async_copy(x_any.at[:, wc:], xnext[0], sems.at[12]))
    for copy in small + copies:
        copy.start()
    for copy in small:
        copy.wait()
    seg = seg_ref[...].astype(f32)
    seg_first = seg[:, 0:1]
    seg_last = [seg[:, (b + 1) * SPAN - 1 : (b + 1) * SPAN] for b in range(nb)]
    eye = iota((hp, hp), 0) == iota((hp, hp), 1)
    rate = jnp.exp(jnp.sum(jnp.where(eye, alog_ref[...], 0.0), axis=1, keepdims=True))
    skip = jnp.sum(jnp.where(eye, skip_ref[...], 0.0), axis=1, keepdims=True)
    dt = dt_ref[...]
    parts = split(dt * (rate * -LOG2E), 3)
    tri = jnp.where(iota((SPAN, SPAN), 0) <= iota((SPAN, SPAN), 1), 1.0, 0.0).astype(bf16)
    sums = mm(jnp.concatenate([parts[:, blk(b)] for b in range(nb)], 0), tri)
    lane = iota((hp, SPAN), 1)
    lane1 = iota((1, SPAN), 1)
    before = jnp.zeros((hp, 1), f32)
    kc = jnp.where(lane == 11, skip, 0.0)
    for b in range(nb):
        three = sums[3 * hp * b : 3 * hp * (b + 1)]
        cum = three[0:hp] + three[hp : 2 * hp] + three[2 * hp :]
        last = cum[:, SPAN - 1 : SPAN]
        segb, dtb = seg[:, blk(b)], dt[:, blk(b)]
        total = cum + before
        rows[0:hp, blk(b)] = cum
        rows[hp : 2 * hp, blk(b)] = jnp.exp2(total) * jnp.where(segb == seg_first, 1.0, 0.0)
        if b > 0:
            rows[2 * hp : 3 * hp, blk(b)] = jnp.exp2(cum) * jnp.where(segb == seg_last[b - 1], 1.0, 0.0)
            keep = jnp.exp2(last) * jnp.where(seg_last[b] == seg_last[b - 1], 1.0, 0.0)
            kc = kc + jnp.where(lane == b, keep, 0.0)
        else:
            rows[2 * hp : 3 * hp, blk(b)] = jnp.zeros((hp, SPAN), f32)
            is_drop = jnp.where((lane1 < KERNEL - 1) & (segb == seg_first), reached(1), 0.0)
            drop = jnp.sum(is_drop, axis=1, keepdims=True)
            early = jnp.exp2(jnp.where(lane < KERNEL - 1, -cum, 0.0)) * dtb * is_drop
            kc = kc + pltpu.roll(early, 8, 1)
        rows[3 * hp : 4 * hp, blk(b)] = jnp.exp2(last - cum) * dtb * jnp.where(segb == seg_last[b], 1.0, 0.0)
        rows[4 * hp : 5 * hp, blk(b)] = cum - jnp.log2(jnp.maximum(dtb, TINY))
        before = before + last
    fend = jnp.exp2(before) * jnp.where(seg_last[-1] == seg_first, 1.0, 0.0)
    kc = kc + jnp.where(lane == 0, fend, 0.0) + jnp.where(lane == 16, drop, 0.0)
    kcols[...] = kc
    delta = iota((SPAN, SPAN), 1) - iota((SPAN, SPAN), 0)
    for b in range(nb):
        segcol = to_column(seg[:, blk(b)])
        same = segcol == seg[:, blk(b)]
        for k in range(KERNEL - 1):
            back = KERNEL - 1 - k
            r = slice(3 * SPAN * b + SPAN * k, 3 * SPAN * b + SPAN * (k + 1))
            shift[r, SPAN:] = jnp.where((delta == -back) & same, 1.0, 0.0).astype(bf16)
            if b > 0:
                same_prev = segcol == seg[:, blk(b - 1)]
                shift[r, 0:SPAN] = jnp.where((delta == SPAN - back) & same_prev, 1.0, 0.0).astype(bf16)
            else:
                shift[r, 0:SPAN] = jnp.zeros((SPAN, SPAN), bf16)
    for copy in copies[:4]:
        copy.wait()
    bchead[...] = bcbuf[0:TAIL, :]
    tb = taps_bc[...] * 0.5
    for b in range(nb):
        if b == 0:
            sh = mm(shift[0 : 3 * SPAN, SPAN:], bcbuf[blk(0), :])
        else:
            sh = mm(shift[3 * SPAN * b : 3 * SPAN * (b + 1), :], bcbuf[(b - 1) * SPAN : (b + 1) * SPAN, :])
        half = sh[0:SPAN] * tb[0:1] + sh[SPAN : 2 * SPAN] * tb[1:2]
        half = half + sh[2 * SPAN :] * tb[2:3] + bcbuf[blk(b), :].astype(f32) * tb[3:4]
        act = silu_from_half(half).astype(bf16)
        bcc[blk(b), :] = act
        bt[:, blk(b)] = act[:, 0:STATE].T
    copies[4].wait()
    chunk_state(
        hp, 0, xbuf, tapx[:, 0:wc] * 0.5, shift, bt, rows, kc, drop, xc, lstate, krows, msg
    )
    for copy in copies[5:]:
        copy.wait()
    lane_last = iota((1, SPAN), 1)
    is_tail = jnp.where((lane_last >= SPAN - (KERNEL - 1)) & (seg[:, blk(nb - 1)] == seg_last[-1]), 1.0, 0.0)
    first_valid = 8.0 - jnp.sum(is_tail, axis=1, keepdims=True)

    def tail_of(value):
        rows8 = value.astype(f32)[8:16]
        return jnp.where(iota(rows8.shape, 0).astype(f32) >= first_valid, rows8, 0.0)

    tile0 = tail_of(xtail[:, 0:wc])
    if nch == 2:
        tile0 = tile0 + pltpu.roll(tail_of(xtail[:, wc:]), 4, 0)
    tile0 = jnp.where(iota(tile0.shape, 0) == 0, seg_last[-1] + 1.0, tile0)
    tail_bc = tail_of(bcbuf[tokens - TAIL :, :])
    tile1 = tail_bc[:, 0:STATE] + pltpu.roll(tail_bc[:, STATE:], 4, 0)
    if wc > STATE:
        tile1 = jnp.concatenate([tile1, jnp.zeros((8, wc - STATE), f32)], 1)
    msg[STATE:, :] = jnp.concatenate([tile0, tile1], 0).astype(bf16)


def next_kernel(hp, first, xbuf, tapx, shift, bt, rows, kcols, msg, xc, lstate, krows):
    wc = xbuf.shape[1]
    chunk_state(
        hp, first, xbuf, tapx[:, wc : 2 * wc] * 0.5, shift, bt, rows, kcols[...],
        kcols[0:1, 16:17], xc, lstate, krows, msg,
    )


def early_conv(halo, head, taps):
    rows = jnp.concatenate([halo, head.astype(f32)[0:8]], 0)
    half = rows[5:13] * taps[0:1]
    for k in range(1, KERNEL):
        half = half + rows[5 + k : 13 + k] * taps[k : k + 1]
    return silu_from_half(half)


def relay_state(krows, recv, b8, xw8, flag):
    base = recv.astype(f32) * flag + mm(b8, xw8, 0, 0)
    return (base * krows[0:1]).astype(bf16)


def relay_first(nch, recv, xhead, bchead, tapx, taps_bc, seg_ref, bcc, *refs):
    krows = refs[:nch]
    out, xw8_ref, x8_ref, b8_ref, c8_ref, flag_ref = refs[nch + 1 :]
    wc = out.shape[1]
    tile = recv[STATE:, :].astype(f32)
    tile0, tile1 = tile[0:8], tile[8:16, 0:STATE]
    seg = seg_ref[:, 0:SPAN].astype(f32)
    seg_first = seg[:, 0:1]
    lane = iota((1, SPAN), 1)
    drop = jnp.sum(
        jnp.where((lane < KERNEL - 1) & (seg == seg_first), reached(1), 0.0), axis=1, keepdims=True
    )
    flag = jnp.where(tile0[0:1, 0:1] == seg_first + 1.0, reached(1), 0.0)
    flag_ref[...] = jnp.broadcast_to(flag, (8, 128))

    def lower(value):
        return jnp.where(iota(value.shape, 0) >= 8 - (KERNEL - 1), value, 0.0) * flag

    def early(value):
        return jnp.where(iota(value.shape, 0).astype(f32) < drop, value, 0.0)

    zero8 = lambda n: jnp.zeros((8, n), f32)
    halo = [lower(tile0)]
    if nch == 2:
        halo.append(lower(pltpu.roll(tile0, 4, 0)))
    bc8 = early_conv(
        jnp.concatenate([lower(tile1), lower(pltpu.roll(tile1, 4, 0))], 1), bchead[...], taps_bc[...] * 0.5
    )
    b8 = jnp.concatenate([early(bc8[:, 0:STATE]), zero8(STATE)], 0).astype(bf16)
    b8_ref[...] = b8
    old = bcc[0:TAIL, STATE:].astype(f32)
    c8 = jnp.where(iota((8, STATE), 0).astype(f32) < drop, bc8[:, STATE:], old[0:8])
    c8_ref[...] = jnp.concatenate([c8, old[8:16]], 0).astype(bf16)
    for c in range(nch):
        cs = slice(c * wc, (c + 1) * wc)
        x8 = early(early_conv(halo[c], xhead[:, cs], tapx[:, cs] * 0.5)).astype(bf16).astype(f32)
        kr = krows[c][...]
        x8_ref[:, cs] = x8 * kr[11:12]
        xw8 = jnp.concatenate([x8 * kr[8:16], zero8(wc)], 0).astype(bf16)
        xw8_ref[:, cs] = xw8
        if c == 0:
            out[...] = relay_state(kr, recv[0:STATE, :], b8, xw8, flag)


def relay_next(recv, krows, b8, xw8, flag, out):
    wc = out.shape[1]
    out[...] = relay_state(krows[...], recv[...], b8[...], xw8[:, wc:], flag[0:1, 0:1])


def inflow_rhs(recv, xw8, flag):
    state = (recv[0:STATE, :].astype(f32) * flag[0:1, 0:1]).astype(bf16)
    return jnp.concatenate([state, xw8, jnp.zeros((128 - TAIL, state.shape[1]), bf16)], 0)


def local_kernel(hp, first, late, *refs):
    z_any, xc, lstate, krows, bcc, bt, rows, seg_ref = refs[:8]
    if late:
        cg, recv, xw8, x8, flag, order = refs[8:14]
    a_ref, q_ref = refs[-5:-3] if not late else refs[-4:-2]
    zbuf, sem = refs[-2:]
    tokens, wc = zbuf.shape
    nb = tokens // SPAN
    lane0 = first * HEAD_DIM
    lanes = slice(lane0, lane0 + wc)
    copy = pltpu.make_async_copy(z_any.at[:, lanes], zbuf, sem)
    copy.start()
    seg = seg_ref[...].astype(f32)
    ex = expander(hp, 2, wc, first)
    head_of = iota((128, SPAN), 0) & (hp - 1)
    low = iota((SPAN, 128), 1) < HEAD_DIM
    tri = iota((SPAN, SPAN), 0) >= iota((SPAN, SPAN), 1)
    if late:
        entering = inflow_rhs(recv, xw8[:, lanes], flag)
    for b in range(nb):
        segcol = to_column(seg[:, blk(b)])
        mask = (segcol == seg[:, blk(b)]) & tri
        c_blk = bcc[blk(b), STATE:]
        scores = jnp.where(mask, mm(c_blk, bt[:, blk(b)]), 0.0)
        scores = jnp.concatenate([scores, scores], 1)
        cum = split(rows[0:hp, blk(b)], 3)
        neg_q = split(-rows[4 * hp : 5 * hp, blk(b)], 3)
        ones = jnp.ones((3 * hp, SPAN), bf16)
        pad = jnp.zeros((128 - 6 * hp, SPAN), bf16)
        left = jnp.concatenate([cum, ones, pad], 0).T
        right = jnp.concatenate([ones, neg_q, pad], 0).astype(f32)
        f_exp = mm(split(rows[hp : 2 * hp, blk(b)], 2), ex, 0, 0)
        if late:
            inflow = mm(cg[blk(b), :], entering)
        if b > 0:
            e_exp = mm(split(rows[2 * hp : 3 * hp, blk(b)], 2), ex, 0, 0)
            carry = mm(c_blk, lstate[blk(b - 1), :])
        if b == 0:
            copy.wait()
        for j in range(wc // 128):
            js = slice(j * 128, (j + 1) * 128)
            xj = xc[blk(b), js]
            h = first + 2 * j
            sel = [jnp.where(head_of == h + i, right, 0.0).astype(bf16) for i in range(2)]
            decay = jnp.exp2(jnp.minimum(mm(left, jnp.concatenate(sel, 1)), 8.0))
            zero = jnp.zeros_like(xj)
            pair = jnp.concatenate([jnp.where(low, xj, zero), jnp.where(low, zero, xj)], 0)
            y = mm((scores * decay).astype(bf16), pair) + xj.astype(f32) * krows[11:12, js]
            if b > 0:
                y = y + e_exp[:, js] * carry[:, js]
            elif late:
                top = y[0:8] + x8[:, lane0 + j * 128 : lane0 + (j + 1) * 128]
                y = jnp.concatenate([top, y[8:]], 0)
            f = f_exp[:, js]
            if late:
                y = y + f * inflow[:, js]
            sz = silu_from_half(zbuf[blk(b), js].astype(f32) * 0.5)
            if b == 0 and not late:
                refs[-3][:, js] = sz[0:8]
            a_ref[blk(b), js] = y * sz
            q_ref[blk(b), js] = f * sz


def rank_kernel(bcc, b8, c8, order, cg):
    tokens = bcc.shape[0]
    b_pad = jnp.concatenate([b8[...], jnp.zeros((128 - TAIL, STATE), bf16)], 0)
    cg[:, 0:STATE] = bcc[:, STATE:]
    cg[0:TAIL, 0:STATE] = c8[...]
    g = mm(cg[:, 0:STATE], b_pad, 1, 1)
    causal = iota((tokens, 128), 0) >= iota((tokens, 128), 1)
    cg[:, STATE:] = jnp.where(causal, g, 0.0).astype(bf16)


def gate_kernel(nrecv, early, *refs):
    cg, flag, a_ref, q_ref, prev = refs[:5]
    recvs, refs = refs[5 : 5 + nrecv], refs[5 + nrecv :]
    gated, sums = refs[-2:]
    tokens, wc = a_ref.shape
    total = None
    if nrecv == 1:
        total = recvs[0][...]
    elif nrecv > 1:
        total = 0.0
        for i, r in enumerate(recvs):
            total = total + r[...].astype(f32) * reached(i + 2)
        total = total.astype(bf16)
    valid = flag[0:1, 0:1] * reached(2)
    if early:
        recv, xw8, x8, sz8 = refs[:4]
        entering = inflow_rhs(recv, xw8[:, 0:wc], flag)
    tile = min(256, wc)
    for b in range(tokens // SPAN):
        acc = None
        for j in range(wc // tile):
            js = slice(j * tile, (j + 1) * tile)
            g = a_ref[blk(b), js]
            if nrecv:
                g = g + (q_ref[blk(b), js] * valid) * mm(cg[blk(b), 0:STATE], total[:, js])
            if early:
                g = g + q_ref[blk(b), js] * mm(cg[blk(b), :], entering[:, js])
                if b == 0:
                    g = jnp.concatenate([g[0:8] + x8[:, js] * sz8[:, js], g[8:]], 0)
            gated[blk(b), js] = g
            sq = g * g
            for i in range(tile // 128):
                part = sq[:, i * 128 : (i + 1) * 128]
                acc = part if acc is None else acc + part
        sums[:, blk(b)] = prev[:, blk(b)] + jnp.sum(acc.T, axis=0, keepdims=True)


def norm_kernel(nch, sums, gain, *refs):
    gated, (out, buf, sems) = refs[:nch], refs[nch:]
    tokens, wc = gated[0].shape
    scale = lax.rsqrt(sums[...] / (HEADS * HEAD_DIM) + 1e-05)
    ones = jnp.ones((48, 128), bf16)
    copies = []
    for b in range(tokens // SPAN):
        wide = jnp.where(iota((16, SPAN), 0) == 0, scale[:, blk(b)], 0.0)
        col = mm(split(wide, 3), ones, 0, 0)
        for c in range(nch):
            for j in range(wc // 128):
                js = slice(j * 128, (j + 1) * 128)
                at = slice(c * wc + j * 128, c * wc + (j + 1) * 128)
                buf[blk(b), at] = (gated[c][blk(b), js] * col * gain[:, at]).astype(bf16)
        copy = pltpu.make_async_copy(buf.at[blk(b), :], out.at[blk(b), :], sems.at[b])
        copy.start()
        copies.append(copy)
    for copy in copies:
        copy.wait()


VMEM = pl.BlockSpec(memory_space=pltpu.VMEM)
ANY = pl.BlockSpec(memory_space=pl.ANY)


def call(body, ins, outs, scratch=(), name=None, limit=24 << 20):
    return pl.pallas_call(
        body,
        out_shape=[pltpu.VMEM(shape, dtype) for shape, dtype in outs],
        in_specs=ins,
        out_specs=[VMEM] * len(outs),
        scratch_shapes=list(scratch),
        compiler_params=pltpu.CompilerParams(vmem_limit_bytes=limit),
        name=name,
    )


def per_device(x_in, z_in, bc_in, conv_x, conv_bc, dt, a_log, skip_d, norm_gain, seg_ids):
    tokens, width = x_in.shape
    heads = dt.shape[0]
    nb = tokens // SPAN
    hp = max(16, heads)
    peers = lax.axis_size("seq")
    rounds = max(1, peers // 2)
    nch = 2 if width % 512 == 0 else 1
    wc = width // nch
    per_chunk = heads // nch
    members = lax.axis_size("head")

    def shift(value, hops):
        return lax.ppermute(value, ("seq", "head"), onward(peers, members, hops - 1))

    if hp != heads:
        dt = jnp.pad(dt, ((0, hp - heads), (0, 0)))
        a_log = jnp.pad(a_log, (0, hp - heads))
        skip_d = jnp.pad(skip_d, (0, hp - heads))
    seg = seg_ids.reshape(1, tokens)
    alog, skip = a_log.reshape(1, hp), skip_d.reshape(1, hp)
    state_outs = [((tokens, wc), bf16), ((SPAN * (nb - 1), wc), bf16), ((16, wc), f32)]
    dma = pltpu.SemaphoreType.DMA
    hbm = lambda value: pltpu.with_memory_space_constraint(value, pltpu.HBM)
    first = call(
        functools.partial(first_kernel, heads, hp, nch),
        [ANY] * 8,
        [((STATE + TAIL, wc), bf16)] + state_outs
        + [
            ((tokens, 2 * STATE), bf16),
            ((STATE, tokens), bf16),
            ((5 * hp, tokens), f32),
            ((hp, 128), f32),
            ((3 * tokens, 2 * SPAN), bf16),
            ((TAIL, width), bf16),
            ((TAIL, 2 * STATE), bf16),
            ((KERNEL, 2 * STATE), f32),
            ((KERNEL, width), f32),
            ((1, tokens), jnp.int32),
        ]
        + [((tokens, wc), bf16)] * (nch - 1),
        [
            pltpu.VMEM((tokens, wc), bf16),
            pltpu.VMEM((tokens, 2 * STATE), bf16),
            pltpu.VMEM((TAIL, width), bf16),
            pltpu.VMEM((hp, tokens), f32),
            pltpu.VMEM((1, hp), f32),
            pltpu.VMEM((1, hp), f32),
            dma((13,)),
        ],
        name="first",
    )
    (
        msg, xc, ls, kr, bcc, bt, rows, kcols, shifts, xhead, bchead, taps_bc, tapx, seg, *xnext
    ) = first(*[hbm(v) for v in (x_in, bc_in, conv_bc, conv_x, dt, alog, skip, seg)])
    xcs, lss, krs = [xc], [ls], [kr]
    recv1 = [shift(msg, 1)]
    if nch == 2:
        msg, xc, ls, kr = call(
            functools.partial(next_kernel, hp, per_chunk),
            [VMEM] * 6,
            [((STATE, wc), bf16)] + state_outs,
            name="next",
        )(xnext[0], tapx, shifts, bt, rows, kcols)
        xcs.append(xc)
        lss.append(ls)
        krs.append(kr)
        recv1.append(shift(msg, 1))
    def run_local(c, extra):
        late = len(extra) > 0
        outs = [((tokens, wc), f32)] * 2 + ([] if late else [((8, wc), f32)])
        return call(
            functools.partial(local_kernel, hp, c * per_chunk, late),
            [ANY] + [VMEM] * (7 + max(0, len(extra) - 1)) + [ANY] * late,
            outs,
            [pltpu.VMEM((tokens, wc), bf16), dma],
            name=f"local{c}",
        )(z_in, xcs[c], lss[c], krs[c], bcc, bt, rows, seg, *extra)

    local = [run_local(0, ())]
    relay, xw8, x8, b8, c8, flag = call(
        functools.partial(relay_first, nch),
        [VMEM] * (7 + nch) + [ANY],
        [
            ((STATE, wc), bf16),
            ((TAIL, width), bf16),
            ((8, width), f32),
            ((TAIL, STATE), bf16),
            ((TAIL, STATE), bf16),
            ((8, 128), f32),
        ],
        name="relay_first",
    )(recv1[0], xhead, bchead, tapx, taps_bc, seg, bcc, *krs, local[0][2])
    later = [[] for c in range(nch)]
    if rounds > 1:
        later[0].append(shift(relay, 2))
    if nch == 2:
        (relay,) = call(relay_next, [VMEM] * 5, [((STATE, wc), bf16)], name="relay_next")(
            recv1[1], krs[1], b8, xw8, flag
        )
        if rounds > 1:
            later[1].append(shift(relay, 2))
    (cg,) = call(rank_kernel, [VMEM] * 3 + [ANY], [((tokens, 2 * STATE), bf16)], name="rank")(
        bcc, b8, c8, relay
    )
    if nch == 2:
        local.append(run_local(1, (cg, recv1[1], xw8, x8, flag, relay)))
    for hops in range(3, rounds + 1):
        for c in range(nch):
            again = later[c][-1].astype(f32) * (krs[c][0:1] * flag[0:1, 0:1] * reached(hops - 1))
            later[c].append(shift(again.astype(bf16), hops))
    sums = jnp.zeros((1, tokens), f32)
    gated = []
    for c in range(nch):
        n = len(later[c])
        a, q, *rest = local[c]
        extra = [recv1[c], xw8, x8, *rest] if rest else []
        g, sums = call(
            functools.partial(gate_kernel, n, len(rest) > 0),
            [VMEM] * (5 + n + len(extra)),
            [((tokens, wc), f32), ((1, tokens), f32)],
            name=f"gate{c}",
        )(cg, flag, a, q, sums, *later[c], *extra)
        gated.append(g)
    swap = lambda step: lax.ppermute(sums, "head", [(i, i ^ step) for i in range(members)])
    step = 1
    while step < members:
        sums = sums + swap(step)
        step *= 2
    return pl.pallas_call(
        functools.partial(norm_kernel, nch),
        out_shape=jax.ShapeDtypeStruct((tokens, width), bf16),
        in_specs=[VMEM] * (2 + nch),
        out_specs=ANY,
        scratch_shapes=[pltpu.VMEM((tokens, width), bf16), dma((nb,))],
        compiler_params=pltpu.CompilerParams(vmem_limit_bytes=24 << 20),
        name="norm",
    )(sums, norm_gain.reshape(1, width), *gated)


def solution(mesh):
    in_specs = (
        P("seq", "head"),
        P("seq", "head"),
        P("seq", None),
        P(None, "head"),
        P(),
        P("head", "seq"),
        P("head"),
        P("head"),
        P("head"),
        P("seq"),
    )
    return jax.shard_map(
        per_device, mesh=mesh, in_specs=in_specs, out_specs=P("seq", "head"), check_vma=False
    )
```

```python
import functools
import jax
import jax.numpy as jnp
from jax import lax
from jax.experimental import pallas as pl
from jax.experimental.pallas import tpu as pltpu
from jax.sharding import PartitionSpec as P

HEADS = 128
HEAD_DIM = 64
STATE = 128
GROUPS = 8
KERNEL = 4
SPAN = 128
LOG2E = 1.4426950408889634
TINY = 1e-37
TAIL = 16
TILE = 512
f32 = jnp.float32
bf16 = jnp.bfloat16


def mm(a, b, ca=1, cb=0):
    return lax.dot_general(a, b, (((ca,), (cb,)), ((), ())), preferred_element_type=f32)


def iota(shape, axis):
    return lax.broadcasted_iota(jnp.int32, shape, axis)


def split(value, parts):
    pieces = []
    for _ in range(parts):
        piece = value.astype(bf16)
        pieces.append(piece)
        value = value - piece.astype(f32)
    return jnp.concatenate(pieces, 0)


def expander(heads, parts, width, first):
    row = iota((parts * heads, width), 0) & (heads - 1)
    col = (iota((parts * heads, width), 1) >> 6) + first
    return jnp.where(row == col, 1.0, 0.0).astype(bf16)


def reached(hops):
    return jnp.where(lax.axis_index("seq") >= hops, 1.0, 0.0)


def onward(peers, members, start):
    moves = []
    for i in range(peers):
        for h in range(members):
            ahead = (i + 1 if i + 1 < peers else start) * members + h
            moves.append((i * members + h, ahead if i >= start else i * members + (h ^ 1)))
    return moves


def silu_from_half(half):
    return half + half * jnp.tanh(half)


def blk(b):
    return slice(b * SPAN, (b + 1) * SPAN)


def to_column(row):
    n = row.shape[1]
    rows = jnp.where(iota((16, n), 0) == 0, row, 0.0).astype(bf16)
    return mm(rows, jnp.ones((16, 128), bf16), 0, 0)


def windows(shift, data, b, js):
    inner = mm(shift[3 * SPAN * b : 3 * SPAN * (b + 1), :], data[blk(b), js])
    if b == 0:
        return inner, None
    at = 3 * data.shape[0] + 3 * TAIL * b
    return inner, mm(shift[at : at + 3 * TAIL, 0:TAIL], data[b * SPAN - TAIL : b * SPAN, js])


def conv_of(sh, data, taps):
    inner, edge = sh
    half = inner[0:SPAN] * taps[0:1] + inner[SPAN : 2 * SPAN] * taps[1:2]
    half = half + inner[2 * SPAN :] * taps[2:3] + data.astype(f32) * taps[3:4]
    if edge is not None:
        top = edge[0:TAIL] * taps[0:1] + edge[TAIL : 2 * TAIL] * taps[1:2]
        half = jnp.concatenate([half[0:TAIL] + (top + edge[2 * TAIL :] * taps[2:3]), half[TAIL:]], 0)
    return silu_from_half(half)


def chunk_state(
    hp, first, x, taps, shift, bt, rows, kcols, drop, xc, lstate, krows, msg, prepare=None
):
    tokens, wc = x.shape
    nb = tokens // SPAN
    kr = mm(split(kcols[:, 0:16], 3), expander(hp, 3, wc, first), 0, 0)
    krows[...] = kr
    tile = min(TILE, wc)
    ex = expander(hp, 2, wc, first)
    steps = [(j, b) for j in range(wc // tile) for b in range(nb)]

    def gather(j, b):
        return windows(shift, x, b, slice(j * tile, (j + 1) * tile))

    ready = gather(*steps[0])
    if prepare is not None:
        prepare()
    to_end = [mm(split(rows[3 * hp : 4 * hp, blk(b)], 2), ex, 0, 0) for b in range(nb)]
    state = None
    for i, (j, b) in enumerate(steps):
        js = slice(j * tile, (j + 1) * tile)
        sh = ready
        if i + 1 < len(steps):
            ready = gather(*steps[i + 1])
        act = conv_of(sh, x[blk(b), js], taps[:, js])
        if b == 0:
            top = act[0:TAIL]
            top = jnp.where(iota(top.shape, 0).astype(f32) < drop, 0.0, top)
            act = jnp.concatenate([top, act[TAIL:]], 0)
        act = act.astype(bf16)
        xc[blk(b), js] = act
        weighted = (act.astype(f32) * to_end[b][:, js]).astype(bf16)
        fresh = mm(bt[:, blk(b)], weighted)
        state = fresh if b == 0 else state * kr[b : b + 1, js] + fresh
        if b < nb - 1:
            lstate[blk(b), js] = state.astype(bf16)
        else:
            msg[0:STATE, js] = state.astype(bf16)


def first_kernel(
    heads, hp, nch,
    x_any, bc_any, tapbc_any, tapx_any, dt_any, alog_any, skip_any, seg_any,
    msg, xc, lstate, krows, bt, rows, kcols, shift, xhead, bchead, taps_bc, tapx, seg_ref, craw,
    last_ref, *refs,
):
    bbuf, xbuf, xtail, dt_ref, alog_ref, skip_ref, sems = refs
    tokens, wc = xbuf.shape
    nb = tokens // SPAN
    group = lax.axis_index("head") * heads // (HEADS // GROUPS)
    col_b = pl.multiple_of(group * STATE, STATE)
    col_c = pl.multiple_of((group + GROUPS) * STATE, STATE)
    width = nch * wc
    small = [(dt_any, dt_ref), (alog_any, alog_ref), (skip_any, skip_ref), (seg_any, seg_ref), (tapx_any, tapx)]
    small = [pltpu.make_async_copy(a, b, sems.at[7 + i]) for i, (a, b) in enumerate(small)]
    copies = [
        pltpu.make_async_copy(bc_any.at[:, pl.ds(col_b, STATE)], bbuf, sems.at[0]),
        pltpu.make_async_copy(bc_any.at[:, pl.ds(col_c, STATE)], craw, sems.at[1]),
        pltpu.make_async_copy(tapbc_any.at[:, pl.ds(col_b, STATE)], taps_bc.at[:, 0:STATE], sems.at[2]),
        pltpu.make_async_copy(tapbc_any.at[:, pl.ds(col_c, STATE)], taps_bc.at[:, STATE:], sems.at[3]),
        pltpu.make_async_copy(x_any.at[:, 0:wc], xbuf, sems.at[4]),
        pltpu.make_async_copy(x_any.at[tokens - TAIL :, :], xtail, sems.at[5]),
        pltpu.make_async_copy(x_any.at[0:TAIL, :], xhead, sems.at[6]),
    ]
    if nch == 2:
        copies.append(pltpu.make_async_copy(x_any.at[:, wc:], last_ref, sems.at[12]))
    for copy in small + copies:
        copy.start()
    for copy in small:
        copy.wait()
    seg = seg_ref[...].astype(f32)
    seg_first = seg[:, 0:1]
    seg_last = [seg[:, (b + 1) * SPAN - 1 : (b + 1) * SPAN] for b in range(nb)]
    eye = iota((hp, hp), 0) == iota((hp, hp), 1)
    rate = jnp.exp(jnp.sum(jnp.where(eye, alog_ref[...], 0.0), axis=1, keepdims=True))
    skip = jnp.sum(jnp.where(eye, skip_ref[...], 0.0), axis=1, keepdims=True)
    dt = dt_ref[...]
    parts = split(dt * (rate * -LOG2E), 3)
    tri = jnp.where(iota((SPAN, SPAN), 0) <= iota((SPAN, SPAN), 1), 1.0, 0.0).astype(bf16)
    sums = mm(jnp.concatenate([parts[:, blk(b)] for b in range(nb)], 0), tri)
    lane = iota((hp, SPAN), 1)
    lane1 = iota((1, SPAN), 1)
    before = jnp.zeros((hp, 1), f32)
    kc = jnp.where(lane == 11, skip, 0.0)
    for b in range(nb):
        three = sums[3 * hp * b : 3 * hp * (b + 1)]
        cum = three[0:hp] + three[hp : 2 * hp] + three[2 * hp :]
        last = cum[:, SPAN - 1 : SPAN]
        segb, dtb = seg[:, blk(b)], dt[:, blk(b)]
        total = cum + before
        rows[0:hp, blk(b)] = cum
        rows[hp : 2 * hp, blk(b)] = jnp.exp2(total) * jnp.where(segb == seg_first, 1.0, 0.0)
        if b > 0:
            rows[2 * hp : 3 * hp, blk(b)] = jnp.exp2(cum) * jnp.where(segb == seg_last[b - 1], 1.0, 0.0)
            keep = jnp.exp2(last) * jnp.where(seg_last[b] == seg_last[b - 1], 1.0, 0.0)
            kc = kc + jnp.where(lane == b, keep, 0.0)
        else:
            rows[2 * hp : 3 * hp, blk(b)] = jnp.zeros((hp, SPAN), f32)
            is_drop = jnp.where((lane1 < KERNEL - 1) & (segb == seg_first), reached(1), 0.0)
            drop = jnp.sum(is_drop, axis=1, keepdims=True)
            early = jnp.exp2(jnp.where(lane < KERNEL - 1, -cum, 0.0)) * dtb * is_drop
            kc = kc + pltpu.roll(early, 8, 1)
        rows[3 * hp : 4 * hp, blk(b)] = jnp.exp2(last - cum) * dtb * jnp.where(segb == seg_last[b], 1.0, 0.0)
        rows[4 * hp : 5 * hp, blk(b)] = cum - jnp.log2(jnp.maximum(dtb, TINY))
        before = before + last
    fend = jnp.exp2(before) * jnp.where(seg_last[-1] == seg_first, 1.0, 0.0)
    kc = kc + jnp.where(lane == 0, fend, 0.0) + jnp.where(lane == 16, drop, 0.0)
    kcols[...] = kc
    delta = iota((SPAN, SPAN), 1) - iota((SPAN, SPAN), 0)
    edge = iota((TAIL, SPAN), 1) - iota((TAIL, SPAN), 0)
    for b in range(nb):
        segcol = to_column(seg[:, blk(b)])
        same = jnp.where(segcol == seg[:, blk(b)], 1.0, 0.0)
        if b > 0:
            past = jnp.concatenate([seg[:, b * SPAN - TAIL : b * SPAN], jnp.zeros((1, SPAN - TAIL), f32)], 1)
            same_past = jnp.where(segcol[0:TAIL] == past, 1.0, 0.0)
        for k in range(KERNEL - 1):
            back = KERNEL - 1 - k
            r = 3 * SPAN * b + SPAN * k
            shift[r : r + SPAN, :] = jnp.where(delta == -back, same, 0.0).astype(bf16)
            if b > 0:
                r = 3 * tokens + TAIL * (3 * b + k)
                shift[r : r + TAIL, :] = jnp.where(edge == TAIL - back, same_past, 0.0).astype(bf16)
    for copy in copies[:5]:
        copy.wait()
    bchead[:, 0:STATE] = bbuf[0:TAIL, :]
    bchead[:, STATE:] = craw[0:TAIL, :]
    every = slice(0, STATE)

    def keys():
        taps = taps_bc[:, 0:STATE] * 0.5
        for b in range(nb):
            bt[:, blk(b)] = conv_of(windows(shift, bbuf, b, every), bbuf[blk(b), :], taps).astype(bf16).T
            if nch == 1:
                queries(shift, craw, taps_bc, last_ref, b)

    chunk_state(
        hp, 0, xbuf, tapx[:, 0:wc] * 0.5, shift, bt, rows, kc, drop, xc, lstate, krows, msg, keys
    )
    for copy in copies[5:]:
        copy.wait()
    lane_last = iota((1, SPAN), 1)
    is_tail = jnp.where((lane_last >= SPAN - (KERNEL - 1)) & (seg[:, blk(nb - 1)] == seg_last[-1]), 1.0, 0.0)
    first_valid = 8.0 - jnp.sum(is_tail, axis=1, keepdims=True)

    def tail_of(value):
        rows8 = value.astype(f32)[8:16]
        return jnp.where(iota(rows8.shape, 0).astype(f32) >= first_valid, rows8, 0.0)

    tile0 = tail_of(xtail[:, 0:wc])
    if nch == 2:
        tile0 = tile0 + pltpu.roll(tail_of(xtail[:, wc:]), 4, 0)
    tile0 = jnp.where(iota(tile0.shape, 0) == 0, seg_last[-1] + 1.0, tile0)
    tile1 = tail_of(bbuf[tokens - TAIL :, :]) + pltpu.roll(tail_of(craw[tokens - TAIL :, :]), 4, 0)
    if wc > STATE:
        tile1 = jnp.concatenate([tile1, jnp.zeros((8, wc - STATE), f32)], 1)
    msg[STATE:, :] = jnp.concatenate([tile0, tile1], 0).astype(bf16)


def queries(shift, craw, taps_bc, cc, b):
    taps = taps_bc[:, STATE:] * 0.5
    sh = windows(shift, craw, b, slice(0, STATE))
    cc[blk(b), :] = conv_of(sh, craw[blk(b), :], taps).astype(bf16)


def next_kernel(
    hp, first, xbuf, tapx, shift, bt, rows, kcols, craw, taps_bc, msg, xc, lstate, krows, cc
):
    wc = xbuf.shape[1]

    def prepare():
        for b in range(xbuf.shape[0] // SPAN):
            queries(shift, craw, taps_bc, cc, b)

    chunk_state(
        hp, first, xbuf, tapx[:, wc : 2 * wc] * 0.5, shift, bt, rows, kcols[...],
        kcols[0:1, 16:17], xc, lstate, krows, msg, prepare,
    )


def early_conv(halo, head, taps):
    rows = jnp.concatenate([halo, head.astype(f32)[0:8]], 0)
    half = rows[5:13] * taps[0:1]
    for k in range(1, KERNEL):
        half = half + rows[5 + k : 13 + k] * taps[k : k + 1]
    return silu_from_half(half)


def relay_state(krows, recv, b8, xw8, flag):
    base = recv.astype(f32) * flag + mm(b8, xw8, 0, 0)
    return (base * krows[0:1]).astype(bf16)


def relay_first(nch, recv, xhead, bchead, tapx, taps_bc, seg_ref, cc, *refs):
    krows = refs[:nch]
    out, xw8_ref, x8_ref, b8_ref, c8_ref, flag_ref = refs[nch + 1 :]
    wc = out.shape[1]
    tile = recv[STATE:, :].astype(f32)
    tile0, tile1 = tile[0:8], tile[8:16, 0:STATE]
    seg = seg_ref[:, 0:SPAN].astype(f32)
    seg_first = seg[:, 0:1]
    lane = iota((1, SPAN), 1)
    drop = jnp.sum(
        jnp.where((lane < KERNEL - 1) & (seg == seg_first), reached(1), 0.0), axis=1, keepdims=True
    )
    flag = jnp.where(tile0[0:1, 0:1] == seg_first + 1.0, reached(1), 0.0)
    flag_ref[...] = jnp.broadcast_to(flag, (8, 128))

    def lower(value):
        return jnp.where(iota(value.shape, 0) >= 8 - (KERNEL - 1), value, 0.0) * flag

    def early(value):
        return jnp.where(iota(value.shape, 0).astype(f32) < drop, value, 0.0)

    zero8 = lambda n: jnp.zeros((8, n), f32)
    halo = [lower(tile0)]
    if nch == 2:
        halo.append(lower(pltpu.roll(tile0, 4, 0)))
    bc8 = early_conv(
        jnp.concatenate([lower(tile1), lower(pltpu.roll(tile1, 4, 0))], 1), bchead[...], taps_bc[...] * 0.5
    )
    b8 = jnp.concatenate([early(bc8[:, 0:STATE]), zero8(STATE)], 0).astype(bf16)
    b8_ref[...] = b8
    old = cc[0:TAIL, :].astype(f32)
    c8 = jnp.where(iota((8, STATE), 0).astype(f32) < drop, bc8[:, STATE:], old[0:8])
    c8_ref[...] = jnp.concatenate([c8, old[8:16]], 0).astype(bf16)
    for c in range(nch):
        cs = slice(c * wc, (c + 1) * wc)
        x8 = early(early_conv(halo[c], xhead[:, cs], tapx[:, cs] * 0.5)).astype(bf16).astype(f32)
        kr = krows[c][...]
        x8_ref[:, cs] = x8 * kr[11:12]
        xw8 = jnp.concatenate([x8 * kr[8:16], zero8(wc)], 0).astype(bf16)
        xw8_ref[:, cs] = xw8
        if c == 0:
            out[...] = relay_state(kr, recv[0:STATE, :], b8, xw8, flag)


def relay_next(recv, krows, b8, xw8, flag, out):
    wc = out.shape[1]
    out[...] = relay_state(krows[...], recv[...], b8[...], xw8[:, wc:], flag[0:1, 0:1])


def inflow_rhs(recv, xw8, flag):
    state = (recv[0:STATE, :].astype(f32) * flag[0:1, 0:1]).astype(bf16)
    return jnp.concatenate([state, xw8, jnp.zeros((128 - TAIL, state.shape[1]), bf16)], 0)


def local_kernel(hp, first, late, *refs):
    z_ref, xc, lstate, krows, cc, bt, rows, seg_ref = refs[:8]
    if late:
        cg, recv, xw8, x8, flag, order = refs[8:14]
    a_ref, q_ref = refs[-2:] if late else refs[-3:-1]
    tokens, wc = a_ref.shape
    nb = tokens // SPAN
    lane0 = first * HEAD_DIM
    lanes = slice(lane0, lane0 + wc)
    seg = seg_ref[...].astype(f32)
    ex = expander(hp, 2, wc, first)
    head_of = iota((128, SPAN), 0) & (hp - 1)
    low = iota((SPAN, 128), 1) < HEAD_DIM
    tri = iota((SPAN, SPAN), 0) >= iota((SPAN, SPAN), 1)
    if late:
        entering = inflow_rhs(recv, xw8[:, lanes], flag)
    for b in range(nb):
        segcol = to_column(seg[:, blk(b)])
        mask = (segcol == seg[:, blk(b)]) & tri
        c_blk = cc[blk(b), :]
        scores = jnp.where(mask, mm(c_blk, bt[:, blk(b)]), 0.0)
        scores = jnp.concatenate([scores, scores], 1)
        cum = split(rows[0:hp, blk(b)], 3)
        neg_q = split(-rows[4 * hp : 5 * hp, blk(b)], 3)
        ones = jnp.ones((3 * hp, SPAN), bf16)
        pad = jnp.zeros((128 - 6 * hp, SPAN), bf16)
        left = jnp.concatenate([cum, ones, pad], 0).T
        right = jnp.concatenate([ones, neg_q, pad], 0).astype(f32)
        f_exp = mm(split(rows[hp : 2 * hp, blk(b)], 2), ex, 0, 0)
        if late:
            inflow = mm(cg[blk(b), :], entering)
        if b > 0:
            e_exp = mm(split(rows[2 * hp : 3 * hp, blk(b)], 2), ex, 0, 0)
            carry = mm(c_blk, lstate[blk(b - 1), :])
        for j in range(wc // 128):
            js = slice(j * 128, (j + 1) * 128)
            xj = xc[blk(b), js]
            h = first + 2 * j
            sel = [jnp.where(head_of == h + i, right, 0.0).astype(bf16) for i in range(2)]
            decay = jnp.exp2(jnp.minimum(mm(left, jnp.concatenate(sel, 1)), 8.0))
            zero = jnp.zeros_like(xj)
            pair = jnp.concatenate([jnp.where(low, xj, zero), jnp.where(low, zero, xj)], 0)
            y = mm((scores * decay).astype(bf16), pair) + xj.astype(f32) * krows[11:12, js]
            if b > 0:
                y = y + e_exp[:, js] * carry[:, js]
            elif late:
                top = y[0:8] + x8[:, lane0 + j * 128 : lane0 + (j + 1) * 128]
                y = jnp.concatenate([top, y[8:]], 0)
            f = f_exp[:, js]
            if late:
                y = y + f * inflow[:, js]
            sz = silu_from_half(z_ref[blk(b), lane0 + j * 128 : lane0 + (j + 1) * 128].astype(f32) * 0.5)
            if b == 0 and not late:
                refs[-1][:, js] = sz[0:8]
            a_ref[blk(b), js] = y * sz
            q_ref[blk(b), js] = f * sz


def rank_kernel(cc, b8, c8, order, cg):
    tokens = cc.shape[0]
    b_pad = jnp.concatenate([b8[...], jnp.zeros((128 - TAIL, STATE), bf16)], 0)
    cg[:, 0:STATE] = cc[...]
    cg[0:TAIL, 0:STATE] = c8[...]
    g = mm(cg[:, 0:STATE], b_pad, 1, 1)
    causal = iota((tokens, 128), 0) >= iota((tokens, 128), 1)
    cg[:, STATE:] = jnp.where(causal, g, 0.0).astype(bf16)


def gate_kernel(nrecv, early, *refs):
    cg, flag, a_ref, q_ref, prev = refs[:5]
    recvs, refs = refs[5 : 5 + nrecv], refs[5 + nrecv :]
    gated, sums = refs[-2:]
    tokens, wc = a_ref.shape
    total = None
    if nrecv == 1:
        total = recvs[0][...]
    elif nrecv > 1:
        total = 0.0
        for i, r in enumerate(recvs):
            total = total + r[...].astype(f32) * reached(i + 2)
        total = total.astype(bf16)
    valid = flag[0:1, 0:1] * reached(2)
    if early:
        recv, xw8, x8, sz8 = refs[:4]
        entering = inflow_rhs(recv, xw8[:, 0:wc], flag)
    tile = min(256, wc)
    for b in range(tokens // SPAN):
        acc = None
        for j in range(wc // tile):
            js = slice(j * tile, (j + 1) * tile)
            g = a_ref[blk(b), js]
            if nrecv:
                g = g + (q_ref[blk(b), js] * valid) * mm(cg[blk(b), 0:STATE], total[:, js])
            if early:
                g = g + q_ref[blk(b), js] * mm(cg[blk(b), :], entering[:, js])
                if b == 0:
                    g = jnp.concatenate([g[0:8] + x8[:, js] * sz8[:, js], g[8:]], 0)
            gated[blk(b), js] = g
            sq = g * g
            for i in range(tile // 128):
                part = sq[:, i * 128 : (i + 1) * 128]
                acc = part if acc is None else acc + part
        sums[:, blk(b)] = prev[:, blk(b)] + jnp.sum(acc.T, axis=0, keepdims=True)


def norm_kernel(nch, sums, gain, *refs):
    gated, (out, buf, sems) = refs[:nch], refs[nch:]
    tokens, wc = gated[0].shape
    scale = lax.rsqrt(sums[...] / (HEADS * HEAD_DIM) + 1e-05)
    ones = jnp.ones((48, 128), bf16)
    copies = []
    for b in range(tokens // SPAN):
        wide = jnp.where(iota((16, SPAN), 0) == 0, scale[:, blk(b)], 0.0)
        col = mm(split(wide, 3), ones, 0, 0)
        for c in range(nch):
            for j in range(wc // 128):
                js = slice(j * 128, (j + 1) * 128)
                at = slice(c * wc + j * 128, c * wc + (j + 1) * 128)
                buf[blk(b), at] = (gated[c][blk(b), js] * col * gain[:, at]).astype(bf16)
        copy = pltpu.make_async_copy(buf.at[blk(b), :], out.at[blk(b), :], sems.at[b])
        copy.start()
        copies.append(copy)
    for copy in copies:
        copy.wait()


VMEM = pl.BlockSpec(memory_space=pltpu.VMEM)
ANY = pl.BlockSpec(memory_space=pl.ANY)


def call(body, ins, outs, scratch=(), name=None, limit=24 << 20):
    return pl.pallas_call(
        body,
        out_shape=[pltpu.VMEM(shape, dtype) for shape, dtype in outs],
        in_specs=ins,
        out_specs=[VMEM] * len(outs),
        scratch_shapes=list(scratch),
        compiler_params=pltpu.CompilerParams(vmem_limit_bytes=limit),
        name=name,
    )


def per_device(x_in, z_in, bc_in, conv_x, conv_bc, dt, a_log, skip_d, norm_gain, seg_ids):
    tokens, width = x_in.shape
    heads = dt.shape[0]
    nb = tokens // SPAN
    hp = max(16, heads)
    peers = lax.axis_size("seq")
    rounds = max(1, peers // 2)
    nch = 2 if width % 512 == 0 else 1
    wc = width // nch
    per_chunk = heads // nch
    members = lax.axis_size("head")

    def shift(value, hops):
        return lax.ppermute(value, ("seq", "head"), onward(peers, members, hops - 1))

    if hp != heads:
        dt = jnp.pad(dt, ((0, hp - heads), (0, 0)))
        a_log = jnp.pad(a_log, (0, hp - heads))
        skip_d = jnp.pad(skip_d, (0, hp - heads))
    seg = seg_ids.reshape(1, tokens)
    alog, skip = a_log.reshape(1, hp), skip_d.reshape(1, hp)
    state_outs = [((tokens, wc), bf16), ((SPAN * (nb - 1), wc), bf16), ((16, wc), f32)]
    dma = pltpu.SemaphoreType.DMA
    hbm = lambda value: pltpu.with_memory_space_constraint(value, pltpu.HBM)
    first = call(
        functools.partial(first_kernel, heads, hp, nch),
        [ANY] * 8,
        [((STATE + TAIL, wc), bf16)] + state_outs
        + [
            ((STATE, tokens), bf16),
            ((5 * hp, tokens), f32),
            ((hp, 128), f32),
            ((3 * (tokens + TAIL * nb), SPAN), bf16),
            ((TAIL, width), bf16),
            ((TAIL, 2 * STATE), bf16),
            ((KERNEL, 2 * STATE), f32),
            ((KERNEL, width), f32),
            ((1, tokens), jnp.int32),
            ((tokens, STATE), bf16),
            ((tokens, wc if nch == 2 else STATE), bf16),
        ],
        [
            pltpu.VMEM((tokens, STATE), bf16),
            pltpu.VMEM((tokens, wc), bf16),
            pltpu.VMEM((TAIL, width), bf16),
            pltpu.VMEM((hp, tokens), f32),
            pltpu.VMEM((1, hp), f32),
            pltpu.VMEM((1, hp), f32),
            dma((13,)),
        ],
        name="first",
    )
    (
        msg, xc, ls, kr, bt, rows, kcols, shifts, xhead, bchead, taps_bc, tapx, seg, craw, cc
    ) = first(*[hbm(v) for v in (x_in, bc_in, conv_bc, conv_x, dt, alog, skip, seg)])
    xcs, lss, krs = [xc], [ls], [kr]
    recv1 = [shift(msg, 1)]
    if nch == 2:
        msg, xc, ls, kr, cc = call(
            functools.partial(next_kernel, hp, per_chunk),
            [VMEM] * 8,
            [((STATE, wc), bf16)] + state_outs + [((tokens, STATE), bf16)],
            name="next",
        )(cc, tapx, shifts, bt, rows, kcols, craw, taps_bc)
        xcs.append(xc)
        lss.append(ls)
        krs.append(kr)
        recv1.append(shift(msg, 1))
    def run_local(c, extra):
        late = len(extra) > 0
        outs = [((tokens, wc), f32)] * 2 + ([] if late else [((8, wc), f32)])
        return call(
            functools.partial(local_kernel, hp, c * per_chunk, late),
            [VMEM] * (8 + max(0, len(extra) - 1)) + [ANY] * late,
            outs,
            name=f"local{c}",
        )(z_in, xcs[c], lss[c], krs[c], cc, bt, rows, seg, *extra)

    local = [run_local(0, ())]
    relay, xw8, x8, b8, c8, flag = call(
        functools.partial(relay_first, nch),
        [VMEM] * (7 + nch) + [ANY],
        [
            ((STATE, wc), bf16),
            ((TAIL, width), bf16),
            ((8, width), f32),
            ((TAIL, STATE), bf16),
            ((TAIL, STATE), bf16),
            ((8, 128), f32),
        ],
        name="relay_first",
    )(recv1[0], xhead, bchead, tapx, taps_bc, seg, cc, *krs, local[0][2])
    later = [[] for c in range(nch)]
    if rounds > 1:
        later[0].append(shift(relay, 2))
    if nch == 2:
        (relay,) = call(relay_next, [VMEM] * 5, [((STATE, wc), bf16)], name="relay_next")(
            recv1[1], krs[1], b8, xw8, flag
        )
        if rounds > 1:
            later[1].append(shift(relay, 2))
    (cg,) = call(rank_kernel, [VMEM] * 3 + [ANY], [((tokens, 2 * STATE), bf16)], name="rank")(
        cc, b8, c8, relay
    )
    if nch == 2:
        local.append(run_local(1, (cg, recv1[1], xw8, x8, flag, relay)))
    for hops in range(3, rounds + 1):
        for c in range(nch):
            again = later[c][-1].astype(f32) * (krs[c][0:1] * flag[0:1, 0:1] * reached(hops - 1))
            later[c].append(shift(again.astype(bf16), hops))
    sums = jnp.zeros((1, tokens), f32)
    gated = []
    for c in range(nch):
        n = len(later[c])
        a, q, *rest = local[c]
        extra = [recv1[c], xw8, x8, *rest] if rest else []
        g, sums = call(
            functools.partial(gate_kernel, n, len(rest) > 0),
            [VMEM] * (5 + n + len(extra)),
            [((tokens, wc), f32), ((1, tokens), f32)],
            name=f"gate{c}",
        )(cg, flag, a, q, sums, *later[c], *extra)
        gated.append(g)
    swap = lambda step: lax.ppermute(sums, "head", [(i, i ^ step) for i in range(members)])
    step = 1
    while step < members:
        sums = sums + swap(step)
        step *= 2
    return pl.pallas_call(
        functools.partial(norm_kernel, nch),
        out_shape=jax.ShapeDtypeStruct((tokens, width), bf16),
        in_specs=[VMEM] * (2 + nch),
        out_specs=ANY,
        scratch_shapes=[pltpu.VMEM((tokens, width), bf16), dma((nb,))],
        compiler_params=pltpu.CompilerParams(vmem_limit_bytes=24 << 20),
        name="norm",
    )(sums, norm_gain.reshape(1, width), *gated)


def solution(mesh):
    in_specs = (
        P("seq", "head"),
        P("seq", "head"),
        P("seq", None),
        P(None, "head"),
        P(),
        P("head", "seq"),
        P("head"),
        P("head"),
        P("head"),
        P("seq"),
    )
    return jax.shard_map(
        per_device, mesh=mesh, in_specs=in_specs, out_specs=P("seq", "head"), check_vma=False
    )
```

```python
import functools
import jax
import jax.numpy as jnp
from jax import lax
from jax.experimental import pallas as pl
from jax.experimental.pallas import tpu as pltpu
from jax.sharding import PartitionSpec as P

HEADS = 128
HEAD_DIM = 64
STATE = 128
GROUPS = 8
KERNEL = 4
SPAN = 128
LOG2E = 1.4426950408889634
TINY = 1e-37
TAIL = 16
TILE = 512
f32 = jnp.float32
bf16 = jnp.bfloat16


def mm(a, b, ca=1, cb=0):
    return lax.dot_general(a, b, (((ca,), (cb,)), ((), ())), preferred_element_type=f32)


def iota(shape, axis):
    return lax.broadcasted_iota(jnp.int32, shape, axis)


def split(value, parts):
    pieces = []
    for _ in range(parts):
        piece = value.astype(bf16)
        pieces.append(piece)
        value = value - piece.astype(f32)
    return jnp.concatenate(pieces, 0)


def expander(heads, parts, width, first):
    row = iota((parts * heads, width), 0) & (heads - 1)
    col = (iota((parts * heads, width), 1) >> 6) + first
    return jnp.where(row == col, 1.0, 0.0).astype(bf16)


def message_rows(wc):
    return STATE + (8 if wc >= 4 * STATE else TAIL)


def reached(hops):
    return jnp.where(lax.axis_index("seq") >= hops, 1.0, 0.0)


def onward(peers, members, start):
    moves = []
    for i in range(peers):
        for h in range(members):
            ahead = (i + 1 if i + 1 < peers else start) * members + h
            moves.append((i * members + h, ahead if i >= start else i * members + (h ^ 1)))
    return moves


def silu_from_half(half):
    return half + half * jnp.tanh(half)


def blk(b):
    return slice(b * SPAN, (b + 1) * SPAN)


def to_column(row):
    n = row.shape[1]
    rows = jnp.where(iota((16, n), 0) == 0, row, 0.0).astype(bf16)
    return mm(rows, jnp.ones((16, 128), bf16), 0, 0)


def windows(shift, data, b, js):
    inner = mm(shift[3 * SPAN * b : 3 * SPAN * (b + 1), :], data[blk(b), js])
    if b == 0:
        return inner, None
    at = 3 * data.shape[0] + 3 * TAIL * b
    return inner, mm(shift[at : at + 3 * TAIL, 0:TAIL], data[b * SPAN - TAIL : b * SPAN, js])


def conv_of(sh, data, taps):
    inner, edge = sh
    half = inner[0:SPAN] * taps[0:1] + inner[SPAN : 2 * SPAN] * taps[1:2]
    half = half + inner[2 * SPAN :] * taps[2:3] + data.astype(f32) * taps[3:4]
    if edge is not None:
        top = edge[0:TAIL] * taps[0:1] + edge[TAIL : 2 * TAIL] * taps[1:2]
        half = jnp.concatenate([half[0:TAIL] + (top + edge[2 * TAIL :] * taps[2:3]), half[TAIL:]], 0)
    return silu_from_half(half)


def chunk_state(
    hp, first, x, taps, shift, bt, rows, kcols, drop, xc, lstate, krows, msg, prepare=None
):
    tokens, wc = x.shape
    nb = tokens // SPAN
    kr = mm(split(kcols[:, 0:16], 3), expander(hp, 3, wc, first), 0, 0)
    krows[...] = kr
    tile = min(TILE, wc)
    ex = expander(hp, 2, wc, first)
    steps = [(j, b) for j in range(wc // tile) for b in range(nb)]

    def gather(j, b):
        return windows(shift, x, b, slice(j * tile, (j + 1) * tile))

    ready = gather(*steps[0])
    if prepare is not None:
        prepare()
    to_end = [mm(split(rows[3 * hp : 4 * hp, blk(b)], 2), ex, 0, 0) for b in range(nb)]
    state = None
    for i, (j, b) in enumerate(steps):
        js = slice(j * tile, (j + 1) * tile)
        sh = ready
        if i + 1 < len(steps):
            ready = gather(*steps[i + 1])
        act = conv_of(sh, x[blk(b), js], taps[:, js])
        if b == 0:
            top = act[0:TAIL]
            top = jnp.where(iota(top.shape, 0).astype(f32) < drop, 0.0, top)
            act = jnp.concatenate([top, act[TAIL:]], 0)
        act = act.astype(bf16)
        xc[blk(b), js] = act
        weighted = (act.astype(f32) * to_end[b][:, js]).astype(bf16)
        fresh = mm(bt[:, blk(b)], weighted)
        state = fresh if b == 0 else state * kr[b : b + 1, js] + fresh
        if b < nb - 1:
            lstate[blk(b), js] = state.astype(bf16)
        else:
            msg[0:STATE, js] = state.astype(bf16)


def first_kernel(
    heads, hp, nch,
    x_any, bc_any, tapbc_any, tapx_any, dt_any, alog_any, skip_any, seg_any,
    msg, xc, lstate, krows, bt, rows, kcols, shift, xhead, bchead, taps_bc, tapx, seg_ref, craw,
    last_ref, *refs,
):
    bbuf, xbuf, xtail, dt_ref, alog_ref, skip_ref, sems = refs
    tokens, wc = xbuf.shape
    nb = tokens // SPAN
    group = lax.axis_index("head") * heads // (HEADS // GROUPS)
    col_b = pl.multiple_of(group * STATE, STATE)
    col_c = pl.multiple_of((group + GROUPS) * STATE, STATE)
    width = nch * wc
    small = [(dt_any, dt_ref), (alog_any, alog_ref), (skip_any, skip_ref), (seg_any, seg_ref), (tapx_any, tapx)]
    small = [pltpu.make_async_copy(a, b, sems.at[7 + i]) for i, (a, b) in enumerate(small)]
    copies = [
        pltpu.make_async_copy(bc_any.at[:, pl.ds(col_b, STATE)], bbuf, sems.at[0]),
        pltpu.make_async_copy(bc_any.at[:, pl.ds(col_c, STATE)], craw, sems.at[1]),
        pltpu.make_async_copy(tapbc_any.at[:, pl.ds(col_b, STATE)], taps_bc.at[:, 0:STATE], sems.at[2]),
        pltpu.make_async_copy(tapbc_any.at[:, pl.ds(col_c, STATE)], taps_bc.at[:, STATE:], sems.at[3]),
        pltpu.make_async_copy(x_any.at[:, 0:wc], xbuf, sems.at[4]),
        pltpu.make_async_copy(x_any.at[tokens - TAIL :, :], xtail, sems.at[5]),
        pltpu.make_async_copy(x_any.at[0:TAIL, :], xhead, sems.at[6]),
    ]
    if nch == 2:
        copies.append(pltpu.make_async_copy(x_any.at[:, wc:], last_ref, sems.at[12]))
    for copy in small + copies:
        copy.start()
    for copy in small:
        copy.wait()
    seg = seg_ref[...].astype(f32)
    seg_first = seg[:, 0:1]
    seg_last = [seg[:, (b + 1) * SPAN - 1 : (b + 1) * SPAN] for b in range(nb)]
    eye = iota((hp, hp), 0) == iota((hp, hp), 1)
    rate = jnp.exp(jnp.sum(jnp.where(eye, alog_ref[...], 0.0), axis=1, keepdims=True))
    skip = jnp.sum(jnp.where(eye, skip_ref[...], 0.0), axis=1, keepdims=True)
    dt = dt_ref[...]
    parts = split(dt * (rate * -LOG2E), 3)
    tri = jnp.where(iota((SPAN, SPAN), 0) <= iota((SPAN, SPAN), 1), 1.0, 0.0).astype(bf16)
    sums = mm(jnp.concatenate([parts[:, blk(b)] for b in range(nb)], 0), tri)
    lane = iota((hp, SPAN), 1)
    lane1 = iota((1, SPAN), 1)
    before = jnp.zeros((hp, 1), f32)
    kc = jnp.where(lane == 11, skip, 0.0)
    for b in range(nb):
        three = sums[3 * hp * b : 3 * hp * (b + 1)]
        cum = three[0:hp] + three[hp : 2 * hp] + three[2 * hp :]
        last = cum[:, SPAN - 1 : SPAN]
        segb, dtb = seg[:, blk(b)], dt[:, blk(b)]
        total = cum + before
        rows[0:hp, blk(b)] = cum
        rows[hp : 2 * hp, blk(b)] = jnp.exp2(total) * jnp.where(segb == seg_first, 1.0, 0.0)
        if b > 0:
            rows[2 * hp : 3 * hp, blk(b)] = jnp.exp2(cum) * jnp.where(segb == seg_last[b - 1], 1.0, 0.0)
            keep = jnp.exp2(last) * jnp.where(seg_last[b] == seg_last[b - 1], 1.0, 0.0)
            kc = kc + jnp.where(lane == b, keep, 0.0)
        else:
            rows[2 * hp : 3 * hp, blk(b)] = jnp.zeros((hp, SPAN), f32)
            is_drop = jnp.where((lane1 < KERNEL - 1) & (segb == seg_first), reached(1), 0.0)
            drop = jnp.sum(is_drop, axis=1, keepdims=True)
            early = jnp.exp2(jnp.where(lane < KERNEL - 1, -cum, 0.0)) * dtb * is_drop
            kc = kc + pltpu.roll(early, 8, 1)
        rows[3 * hp : 4 * hp, blk(b)] = jnp.exp2(last - cum) * dtb * jnp.where(segb == seg_last[b], 1.0, 0.0)
        rows[4 * hp : 5 * hp, blk(b)] = cum - jnp.log2(jnp.maximum(dtb, TINY))
        before = before + last
    fend = jnp.exp2(before) * jnp.where(seg_last[-1] == seg_first, 1.0, 0.0)
    kc = kc + jnp.where(lane == 0, fend, 0.0) + jnp.where(lane == 16, drop, 0.0)
    kcols[...] = kc
    delta = iota((SPAN, SPAN), 1) - iota((SPAN, SPAN), 0)
    edge = iota((TAIL, SPAN), 1) - iota((TAIL, SPAN), 0)
    for b in range(nb):
        segcol = to_column(seg[:, blk(b)])
        same = jnp.where(segcol == seg[:, blk(b)], 1.0, 0.0)
        if b > 0:
            past = jnp.concatenate([seg[:, b * SPAN - TAIL : b * SPAN], jnp.zeros((1, SPAN - TAIL), f32)], 1)
            same_past = jnp.where(segcol[0:TAIL] == past, 1.0, 0.0)
        for k in range(KERNEL - 1):
            back = KERNEL - 1 - k
            r = 3 * SPAN * b + SPAN * k
            shift[r : r + SPAN, :] = jnp.where(delta == -back, same, 0.0).astype(bf16)
            if b > 0:
                r = 3 * tokens + TAIL * (3 * b + k)
                shift[r : r + TAIL, :] = jnp.where(edge == TAIL - back, same_past, 0.0).astype(bf16)
    for copy in copies[:5]:
        copy.wait()
    bchead[:, 0:STATE] = bbuf[0:TAIL, :]
    bchead[:, STATE:] = craw[0:TAIL, :]
    every = slice(0, STATE)

    def keys():
        taps = taps_bc[:, 0:STATE] * 0.5
        for b in range(nb):
            bt[:, blk(b)] = conv_of(windows(shift, bbuf, b, every), bbuf[blk(b), :], taps).astype(bf16).T
            if nch == 1:
                queries(shift, craw, taps_bc, last_ref, b)

    chunk_state(
        hp, 0, xbuf, tapx[:, 0:wc] * 0.5, shift, bt, rows, kc, drop, xc, lstate, krows, msg, keys
    )
    for copy in copies[5:]:
        copy.wait()
    lane_last = iota((1, SPAN), 1)
    is_tail = jnp.where((lane_last >= SPAN - (KERNEL - 1)) & (seg[:, blk(nb - 1)] == seg_last[-1]), 1.0, 0.0)
    first_valid = 8.0 - jnp.sum(is_tail, axis=1, keepdims=True)

    def tail_of(value):
        rows8 = value.astype(f32)[8:16]
        return jnp.where(iota(rows8.shape, 0).astype(f32) >= first_valid, rows8, 0.0)

    tile0 = tail_of(xtail[:, 0:wc])
    if nch == 2:
        tile0 = tile0 + pltpu.roll(tail_of(xtail[:, wc:]), 4, 0)
    tail_b, tail_c = tail_of(bbuf[tokens - TAIL :, :]), tail_of(craw[tokens - TAIL :, :])
    if message_rows(wc) == STATE + 8:
        row0 = jnp.concatenate([tail_b[5:6], tail_c[5:6], tail_b[6:7], tail_c[6:7]], 1)
        mark = jnp.broadcast_to(seg_last[-1] + 1.0, (1, STATE))
        row4 = jnp.concatenate([tail_b[7:8], tail_c[7:8], mark, mark], 1)
        if wc > 4 * STATE:
            rest = jnp.zeros((1, wc - 4 * STATE), f32)
            row0, row4 = (jnp.concatenate([r, rest], 1) for r in (row0, row4))
        row = iota(tile0.shape, 0)
        tile0 = jnp.where(row == 0, row0, jnp.where(row == 4, row4, tile0))
        msg[STATE:, :] = tile0.astype(bf16)
        return
    tile0 = jnp.where(iota(tile0.shape, 0) == 0, seg_last[-1] + 1.0, tile0)
    tile1 = tail_b + pltpu.roll(tail_c, 4, 0)
    if wc > STATE:
        tile1 = jnp.concatenate([tile1, jnp.zeros((8, wc - STATE), f32)], 1)
    msg[STATE:, :] = jnp.concatenate([tile0, tile1], 0).astype(bf16)


def queries(shift, craw, taps_bc, cc, b):
    taps = taps_bc[:, STATE:] * 0.5
    sh = windows(shift, craw, b, slice(0, STATE))
    cc[blk(b), :] = conv_of(sh, craw[blk(b), :], taps).astype(bf16)


def next_kernel(
    hp, first, xbuf, tapx, shift, bt, rows, kcols, craw, taps_bc, msg, xc, lstate, krows, cc
):
    wc = xbuf.shape[1]

    def prepare():
        for b in range(xbuf.shape[0] // SPAN):
            queries(shift, craw, taps_bc, cc, b)

    chunk_state(
        hp, first, xbuf, tapx[:, wc : 2 * wc] * 0.5, shift, bt, rows, kcols[...],
        kcols[0:1, 16:17], xc, lstate, krows, msg, prepare,
    )


def early_conv(halo, head, taps):
    rows = jnp.concatenate([halo, head.astype(f32)[0:8]], 0)
    half = rows[5:13] * taps[0:1]
    for k in range(1, KERNEL):
        half = half + rows[5 + k : 13 + k] * taps[k : k + 1]
    return silu_from_half(half)


def relay_state(krows, recv, b8, xw8, flag):
    base = recv.astype(f32) * flag + mm(b8, xw8, 0, 0)
    return (base * krows[0:1]).astype(bf16)


def relay_first(nch, recv, xhead, bchead, tapx, taps_bc, seg_ref, cc, *refs):
    krows = refs[:nch]
    out, xw8_ref, x8_ref, b8_ref, c8_ref, flag_ref = refs[nch + 1 :]
    wc = out.shape[1]
    tile = recv[STATE:, :].astype(f32)
    tile0 = tile[0:8]
    mark = tile0[0:1, 0:1]
    if message_rows(wc) == STATE + 8:
        row = iota((8, STATE), 0)

        def three(at):
            first, second = tile0[0:1, at : at + STATE], tile0[0:1, at + 2 * STATE : at + 3 * STATE]
            third = jnp.where(row == 7, tile0[4:5, at : at + STATE], 0.0)
            return jnp.where(row == 5, first, jnp.where(row == 6, second, third))

        mark = tile0[4:5, 2 * STATE : 2 * STATE + 1]
        tail_b, tail_c = three(0), three(STATE)
    else:
        tail_b, tail_c = tile[8:16, 0:STATE], pltpu.roll(tile[8:16, 0:STATE], 4, 0)
    seg = seg_ref[:, 0:SPAN].astype(f32)
    seg_first = seg[:, 0:1]
    lane = iota((1, SPAN), 1)
    drop = jnp.sum(
        jnp.where((lane < KERNEL - 1) & (seg == seg_first), reached(1), 0.0), axis=1, keepdims=True
    )
    flag = jnp.where(mark == seg_first + 1.0, reached(1), 0.0)
    flag_ref[...] = jnp.broadcast_to(flag, (8, 128))

    def lower(value):
        return jnp.where(iota(value.shape, 0) >= 8 - (KERNEL - 1), value, 0.0) * flag

    def early(value):
        return jnp.where(iota(value.shape, 0).astype(f32) < drop, value, 0.0)

    zero8 = lambda n: jnp.zeros((8, n), f32)
    halo = [lower(tile0)]
    if nch == 2:
        halo.append(lower(pltpu.roll(tile0, 4, 0)))
    bc8 = early_conv(
        jnp.concatenate([lower(tail_b), lower(tail_c)], 1), bchead[...], taps_bc[...] * 0.5
    )
    b8 = jnp.concatenate([early(bc8[:, 0:STATE]), zero8(STATE)], 0).astype(bf16)
    b8_ref[...] = b8
    old = cc[0:TAIL, :].astype(f32)
    c8 = jnp.where(iota((8, STATE), 0).astype(f32) < drop, bc8[:, STATE:], old[0:8])
    c8_ref[...] = jnp.concatenate([c8, old[8:16]], 0).astype(bf16)
    for c in range(nch):
        cs = slice(c * wc, (c + 1) * wc)
        x8 = early(early_conv(halo[c], xhead[:, cs], tapx[:, cs] * 0.5)).astype(bf16).astype(f32)
        kr = krows[c][...]
        x8_ref[:, cs] = x8 * kr[11:12]
        xw8 = jnp.concatenate([x8 * kr[8:16], zero8(wc)], 0).astype(bf16)
        xw8_ref[:, cs] = xw8
        if c == 0:
            out[...] = relay_state(kr, recv[0:STATE, :], b8, xw8, flag)


def relay_next(recv, krows, b8, xw8, flag, out):
    wc = out.shape[1]
    out[...] = relay_state(krows[...], recv[...], b8[...], xw8[:, wc:], flag[0:1, 0:1])


def inflow_rhs(recv, xw8, flag):
    state = (recv[0:STATE, :].astype(f32) * flag[0:1, 0:1]).astype(bf16)
    return jnp.concatenate([state, xw8, jnp.zeros((128 - TAIL, state.shape[1]), bf16)], 0)


def local_kernel(hp, first, late, *refs):
    z_ref, xc, lstate, krows, cc, bt, rows, seg_ref = refs[:8]
    if late:
        cg, recv, xw8, x8, flag, order = refs[8:14]
    a_ref, q_ref = refs[-2:] if late else refs[-3:-1]
    tokens, wc = a_ref.shape
    nb = tokens // SPAN
    lane0 = first * HEAD_DIM
    lanes = slice(lane0, lane0 + wc)
    seg = seg_ref[...].astype(f32)
    ex = expander(hp, 2, wc, first)
    head_of = iota((128, SPAN), 0) & (hp - 1)
    low = iota((SPAN, 128), 1) < HEAD_DIM
    tri = iota((SPAN, SPAN), 0) >= iota((SPAN, SPAN), 1)
    if late:
        entering = inflow_rhs(recv, xw8[:, lanes], flag)
    for b in range(nb):
        segcol = to_column(seg[:, blk(b)])
        mask = (segcol == seg[:, blk(b)]) & tri
        c_blk = cc[blk(b), :]
        scores = jnp.where(mask, mm(c_blk, bt[:, blk(b)]), 0.0)
        scores = jnp.concatenate([scores, scores], 1)
        cum = split(rows[0:hp, blk(b)], 3)
        neg_q = split(-rows[4 * hp : 5 * hp, blk(b)], 3)
        ones = jnp.ones((3 * hp, SPAN), bf16)
        pad = jnp.zeros((128 - 6 * hp, SPAN), bf16)
        left = jnp.concatenate([cum, ones, pad], 0).T
        right = jnp.concatenate([ones, neg_q, pad], 0).astype(f32)
        f_exp = mm(split(rows[hp : 2 * hp, blk(b)], 2), ex, 0, 0)
        if late:
            inflow = mm(cg[blk(b), :], entering)
        if b > 0:
            e_exp = mm(split(rows[2 * hp : 3 * hp, blk(b)], 2), ex, 0, 0)
            carry = mm(c_blk, lstate[blk(b - 1), :])
        for j in range(wc // 128):
            js = slice(j * 128, (j + 1) * 128)
            xj = xc[blk(b), js]
            h = first + 2 * j
            sel = [jnp.where(head_of == h + i, right, 0.0).astype(bf16) for i in range(2)]
            decay = jnp.exp2(jnp.minimum(mm(left, jnp.concatenate(sel, 1)), 8.0))
            zero = jnp.zeros_like(xj)
            pair = jnp.concatenate([jnp.where(low, xj, zero), jnp.where(low, zero, xj)], 0)
            y = mm((scores * decay).astype(bf16), pair) + xj.astype(f32) * krows[11:12, js]
            if b > 0:
                y = y + e_exp[:, js] * carry[:, js]
            elif late:
                top = y[0:8] + x8[:, lane0 + j * 128 : lane0 + (j + 1) * 128]
                y = jnp.concatenate([top, y[8:]], 0)
            f = f_exp[:, js]
            if late:
                y = y + f * inflow[:, js]
            sz = silu_from_half(z_ref[blk(b), lane0 + j * 128 : lane0 + (j + 1) * 128].astype(f32) * 0.5)
            if b == 0 and not late:
                refs[-1][:, js] = sz[0:8]
            a_ref[blk(b), js] = y * sz
            q_ref[blk(b), js] = f * sz


def rank_kernel(cc, b8, c8, order, cg):
    tokens = cc.shape[0]
    b_pad = jnp.concatenate([b8[...], jnp.zeros((128 - TAIL, STATE), bf16)], 0)
    cg[:, 0:STATE] = cc[...]
    cg[0:TAIL, 0:STATE] = c8[...]
    g = mm(cg[:, 0:STATE], b_pad, 1, 1)
    causal = iota((tokens, 128), 0) >= iota((tokens, 128), 1)
    cg[:, STATE:] = jnp.where(causal, g, 0.0).astype(bf16)


def gate_kernel(nrecv, early, *refs):
    cg, flag, a_ref, q_ref, prev = refs[:5]
    recvs, refs = refs[5 : 5 + nrecv], refs[5 + nrecv :]
    gated, sums = refs[-2:]
    tokens, wc = a_ref.shape
    total = None
    if nrecv == 1:
        total = recvs[0][...]
    elif nrecv > 1:
        total = 0.0
        for i, r in enumerate(recvs):
            total = total + r[...].astype(f32) * reached(i + 2)
        total = total.astype(bf16)
    valid = flag[0:1, 0:1] * reached(2)
    if early:
        recv, xw8, x8, sz8 = refs[:4]
        entering = inflow_rhs(recv, xw8[:, 0:wc], flag)
    tile = min(256, wc)
    for b in range(tokens // SPAN):
        acc = None
        for j in range(wc // tile):
            js = slice(j * tile, (j + 1) * tile)
            g = a_ref[blk(b), js]
            if nrecv:
                g = g + (q_ref[blk(b), js] * valid) * mm(cg[blk(b), 0:STATE], total[:, js])
            if early:
                g = g + q_ref[blk(b), js] * mm(cg[blk(b), :], entering[:, js])
                if b == 0:
                    g = jnp.concatenate([g[0:8] + x8[:, js] * sz8[:, js], g[8:]], 0)
            gated[blk(b), js] = g
            sq = g * g
            for i in range(tile // 128):
                part = sq[:, i * 128 : (i + 1) * 128]
                acc = part if acc is None else acc + part
        sums[:, blk(b)] = prev[:, blk(b)] + jnp.sum(acc.T, axis=0, keepdims=True)


def norm_kernel(nch, sums, gain, *refs):
    gated, (out, buf, sems) = refs[:nch], refs[nch:]
    tokens, wc = gated[0].shape
    scale = lax.rsqrt(sums[...] / (HEADS * HEAD_DIM) + 1e-05)
    ones = jnp.ones((48, 128), bf16)
    copies = []
    for b in range(tokens // SPAN):
        wide = jnp.where(iota((16, SPAN), 0) == 0, scale[:, blk(b)], 0.0)
        col = mm(split(wide, 3), ones, 0, 0)
        for c in range(nch):
            for j in range(wc // 128):
                js = slice(j * 128, (j + 1) * 128)
                at = slice(c * wc + j * 128, c * wc + (j + 1) * 128)
                buf[blk(b), at] = (gated[c][blk(b), js] * col * gain[:, at]).astype(bf16)
        copy = pltpu.make_async_copy(buf.at[blk(b), :], out.at[blk(b), :], sems.at[b])
        copy.start()
        copies.append(copy)
    for copy in copies:
        copy.wait()


VMEM = pl.BlockSpec(memory_space=pltpu.VMEM)
ANY = pl.BlockSpec(memory_space=pl.ANY)


def call(body, ins, outs, scratch=(), name=None, limit=24 << 20):
    return pl.pallas_call(
        body,
        out_shape=[pltpu.VMEM(shape, dtype) for shape, dtype in outs],
        in_specs=ins,
        out_specs=[VMEM] * len(outs),
        scratch_shapes=list(scratch),
        compiler_params=pltpu.CompilerParams(vmem_limit_bytes=limit),
        name=name,
    )


def per_device(x_in, z_in, bc_in, conv_x, conv_bc, dt, a_log, skip_d, norm_gain, seg_ids):
    tokens, width = x_in.shape
    heads = dt.shape[0]
    nb = tokens // SPAN
    hp = max(16, heads)
    peers = lax.axis_size("seq")
    rounds = max(1, peers // 2)
    nch = 2 if width % 512 == 0 else 1
    wc = width // nch
    per_chunk = heads // nch
    members = lax.axis_size("head")

    def shift(value, hops):
        return lax.ppermute(value, ("seq", "head"), onward(peers, members, hops - 1))

    if hp != heads:
        dt = jnp.pad(dt, ((0, hp - heads), (0, 0)))
        a_log = jnp.pad(a_log, (0, hp - heads))
        skip_d = jnp.pad(skip_d, (0, hp - heads))
    seg = seg_ids.reshape(1, tokens)
    alog, skip = a_log.reshape(1, hp), skip_d.reshape(1, hp)
    state_outs = [((tokens, wc), bf16), ((SPAN * (nb - 1), wc), bf16), ((16, wc), f32)]
    dma = pltpu.SemaphoreType.DMA
    hbm = lambda value: pltpu.with_memory_space_constraint(value, pltpu.HBM)
    first = call(
        functools.partial(first_kernel, heads, hp, nch),
        [ANY] * 8,
        [((message_rows(wc), wc), bf16)] + state_outs
        + [
            ((STATE, tokens), bf16),
            ((5 * hp, tokens), f32),
            ((hp, 128), f32),
            ((3 * (tokens + TAIL * nb), SPAN), bf16),
            ((TAIL, width), bf16),
            ((TAIL, 2 * STATE), bf16),
            ((KERNEL, 2 * STATE), f32),
            ((KERNEL, width), f32),
            ((1, tokens), jnp.int32),
            ((tokens, STATE), bf16),
            ((tokens, wc if nch == 2 else STATE), bf16),
        ],
        [
            pltpu.VMEM((tokens, STATE), bf16),
            pltpu.VMEM((tokens, wc), bf16),
            pltpu.VMEM((TAIL, width), bf16),
            pltpu.VMEM((hp, tokens), f32),
            pltpu.VMEM((1, hp), f32),
            pltpu.VMEM((1, hp), f32),
            dma((13,)),
        ],
        name="first",
    )
    (
        msg, xc, ls, kr, bt, rows, kcols, shifts, xhead, bchead, taps_bc, tapx, seg, craw, cc
    ) = first(*[hbm(v) for v in (x_in, bc_in, conv_bc, conv_x, dt, alog, skip, seg)])
    xcs, lss, krs = [xc], [ls], [kr]
    recv1 = [shift(msg, 1)]
    if nch == 2:
        msg, xc, ls, kr, cc = call(
            functools.partial(next_kernel, hp, per_chunk),
            [VMEM] * 8,
            [((STATE, wc), bf16)] + state_outs + [((tokens, STATE), bf16)],
            name="next",
        )(cc, tapx, shifts, bt, rows, kcols, craw, taps_bc)
        xcs.append(xc)
        lss.append(ls)
        krs.append(kr)
        recv1.append(shift(msg, 1))
    def run_local(c, extra):
        late = len(extra) > 0
        outs = [((tokens, wc), f32)] * 2 + ([] if late else [((8, wc), f32)])
        return call(
            functools.partial(local_kernel, hp, c * per_chunk, late),
            [VMEM] * (8 + max(0, len(extra) - 1)) + [ANY] * late,
            outs,
            name=f"local{c}",
        )(z_in, xcs[c], lss[c], krs[c], cc, bt, rows, seg, *extra)

    local = [run_local(0, ())]
    relay, xw8, x8, b8, c8, flag = call(
        functools.partial(relay_first, nch),
        [VMEM] * (7 + nch) + [ANY],
        [
            ((STATE, wc), bf16),
            ((TAIL, width), bf16),
            ((8, width), f32),
            ((TAIL, STATE), bf16),
            ((TAIL, STATE), bf16),
            ((8, 128), f32),
        ],
        name="relay_first",
    )(recv1[0], xhead, bchead, tapx, taps_bc, seg, cc, *krs, local[0][2])
    later = [[] for c in range(nch)]
    if rounds > 1:
        later[0].append(shift(relay, 2))
    if nch == 2:
        (relay,) = call(relay_next, [VMEM] * 5, [((STATE, wc), bf16)], name="relay_next")(
            recv1[1], krs[1], b8, xw8, flag
        )
        if rounds > 1:
            later[1].append(shift(relay, 2))
    (cg,) = call(rank_kernel, [VMEM] * 3 + [ANY], [((tokens, 2 * STATE), bf16)], name="rank")(
        cc, b8, c8, relay
    )
    if nch == 2:
        local.append(run_local(1, (cg, recv1[1], xw8, x8, flag, relay)))
    for hops in range(3, rounds + 1):
        for c in range(nch):
            again = later[c][-1].astype(f32) * (krs[c][0:1] * flag[0:1, 0:1] * reached(hops - 1))
            later[c].append(shift(again.astype(bf16), hops))
    sums = jnp.zeros((1, tokens), f32)
    gated = []
    for c in range(nch):
        n = len(later[c])
        a, q, *rest = local[c]
        extra = [recv1[c], xw8, x8, *rest] if rest else []
        g, sums = call(
            functools.partial(gate_kernel, n, len(rest) > 0),
            [VMEM] * (5 + n + len(extra)),
            [((tokens, wc), f32), ((1, tokens), f32)],
            name=f"gate{c}",
        )(cg, flag, a, q, sums, *later[c], *extra)
        gated.append(g)
    swap = lambda step: lax.ppermute(sums, "head", [(i, i ^ step) for i in range(members)])
    step = 1
    while step < members:
        sums = sums + swap(step)
        step *= 2
    return pl.pallas_call(
        functools.partial(norm_kernel, nch),
        out_shape=jax.ShapeDtypeStruct((tokens, width), bf16),
        in_specs=[VMEM] * (2 + nch),
        out_specs=ANY,
        scratch_shapes=[pltpu.VMEM((tokens, width), bf16), dma((nb,))],
        compiler_params=pltpu.CompilerParams(vmem_limit_bytes=24 << 20),
        name="norm",
    )(sums, norm_gain.reshape(1, width), *gated)


def solution(mesh):
    in_specs = (
        P("seq", "head"),
        P("seq", "head"),
        P("seq", None),
        P(None, "head"),
        P(),
        P("head", "seq"),
        P("head"),
        P("head"),
        P("head"),
        P("seq"),
    )
    return jax.shard_map(
        per_device, mesh=mesh, in_specs=in_specs, out_specs=P("seq", "head"), check_vma=False
    )
```

```python
import functools
import jax
import jax.numpy as jnp
from jax import lax
from jax.experimental import pallas as pl
from jax.experimental.pallas import tpu as pltpu
from jax.sharding import PartitionSpec as P

HEADS = 128
HEAD_DIM = 64
STATE = 128
GROUPS = 8
KERNEL = 4
SPAN = 128
LOG2E = 1.4426950408889634
TINY = 1e-37
TAIL = 16
TILE = 512
f32 = jnp.float32
bf16 = jnp.bfloat16


def mm(a, b, ca=1, cb=0):
    return lax.dot_general(a, b, (((ca,), (cb,)), ((), ())), preferred_element_type=f32)


def iota(shape, axis):
    return lax.broadcasted_iota(jnp.int32, shape, axis)


def split(value, parts):
    pieces = []
    for _ in range(parts):
        piece = value.astype(bf16)
        pieces.append(piece)
        value = value - piece.astype(f32)
    return jnp.concatenate(pieces, 0)


def expander(heads, parts, width, first):
    row = iota((parts * heads, width), 0) & (heads - 1)
    col = (iota((parts * heads, width), 1) >> 6) + first
    return jnp.where(row == col, 1.0, 0.0).astype(bf16)


def message_rows(wc):
    return STATE + (8 if wc >= 4 * STATE else TAIL)


def reached(hops):
    return jnp.where(lax.axis_index("seq") >= hops, 1.0, 0.0)


def onward(peers, members, start):
    moves = []
    for i in range(peers):
        for h in range(members):
            ahead = (i + 1 if i + 1 < peers else start) * members + h
            moves.append((i * members + h, ahead if i >= start else i * members + (h ^ 1)))
    return moves


def silu_from_half(half):
    return half + half * jnp.tanh(half)


def blk(b):
    return slice(b * SPAN, (b + 1) * SPAN)


def to_column(row):
    n = row.shape[1]
    rows = jnp.where(iota((16, n), 0) == 0, row, 0.0).astype(bf16)
    return mm(rows, jnp.ones((16, 128), bf16), 0, 0)


def windows(shift, data, b, js):
    inner = mm(shift[3 * SPAN * b : 3 * SPAN * (b + 1), :], data[blk(b), js])
    if b == 0:
        return inner, None
    at = 3 * data.shape[0] + 3 * TAIL * b
    return inner, mm(shift[at : at + 3 * TAIL, 0:TAIL], data[b * SPAN - TAIL : b * SPAN, js])


def conv_of(sh, data, taps):
    inner, edge = sh
    half = inner[0:SPAN] * taps[0:1] + inner[SPAN : 2 * SPAN] * taps[1:2]
    half = half + inner[2 * SPAN :] * taps[2:3] + data.astype(f32) * taps[3:4]
    if edge is not None:
        top = edge[0:TAIL] * taps[0:1] + edge[TAIL : 2 * TAIL] * taps[1:2]
        half = jnp.concatenate([half[0:TAIL] + (top + edge[2 * TAIL :] * taps[2:3]), half[TAIL:]], 0)
    return silu_from_half(half)


def chunk_state(
    hp, first, x, taps, shift, bt, rows, kcols, drop, xc, lstate, krows, msg, prepare=None
):
    tokens, wc = x.shape
    nb = tokens // SPAN
    kr = mm(split(kcols[:, 0:16], 3), expander(hp, 3, wc, first), 0, 0)
    krows[...] = kr
    tile = min(TILE, wc)
    ex = expander(hp, 2, wc, first)
    steps = [(j, b) for j in range(wc // tile) for b in range(nb)]

    def gather(j, b):
        return windows(shift, x, b, slice(j * tile, (j + 1) * tile))

    ready = [gather(*step) for step in steps[:2]]
    if prepare is not None:
        prepare()
    to_end = [mm(split(rows[3 * hp : 4 * hp, blk(b)], 2), ex, 0, 0) for b in range(nb)]
    state = None
    for i, (j, b) in enumerate(steps):
        js = slice(j * tile, (j + 1) * tile)
        sh = ready.pop(0)
        if i + 2 < len(steps):
            ready.append(gather(*steps[i + 2]))
        act = conv_of(sh, x[blk(b), js], taps[:, js])
        if b == 0:
            top = act[0:TAIL]
            top = jnp.where(iota(top.shape, 0).astype(f32) < drop, 0.0, top)
            act = jnp.concatenate([top, act[TAIL:]], 0)
        act = act.astype(bf16)
        xc[blk(b), js] = act
        weighted = (act.astype(f32) * to_end[b][:, js]).astype(bf16)
        fresh = mm(bt[:, blk(b)], weighted)
        state = fresh if b == 0 else state * kr[b : b + 1, js] + fresh
        if b < nb - 1:
            lstate[blk(b), js] = state.astype(bf16)
        else:
            msg[0:STATE, js] = state.astype(bf16)


def first_kernel(
    heads, hp, nch,
    x_any, bc_any, tapbc_any, tapx_any, dt_any, alog_any, skip_any, seg_any,
    msg, xc, lstate, krows, bt, rows, kcols, shift, xhead, bchead, taps_bc, tapx, seg_ref, craw,
    last_ref, *refs,
):
    bbuf, xbuf, xtail, dt_ref, alog_ref, skip_ref, sems = refs
    tokens, wc = xbuf.shape
    nb = tokens // SPAN
    group = lax.axis_index("head") * heads // (HEADS // GROUPS)
    col_b = pl.multiple_of(group * STATE, STATE)
    col_c = pl.multiple_of((group + GROUPS) * STATE, STATE)
    width = nch * wc
    small = [(dt_any, dt_ref), (alog_any, alog_ref), (skip_any, skip_ref), (seg_any, seg_ref), (tapx_any, tapx)]
    small = [pltpu.make_async_copy(a, b, sems.at[7 + i]) for i, (a, b) in enumerate(small)]
    copies = [
        pltpu.make_async_copy(bc_any.at[:, pl.ds(col_b, STATE)], bbuf, sems.at[0]),
        pltpu.make_async_copy(bc_any.at[:, pl.ds(col_c, STATE)], craw, sems.at[1]),
        pltpu.make_async_copy(tapbc_any.at[:, pl.ds(col_b, STATE)], taps_bc.at[:, 0:STATE], sems.at[2]),
        pltpu.make_async_copy(tapbc_any.at[:, pl.ds(col_c, STATE)], taps_bc.at[:, STATE:], sems.at[3]),
        pltpu.make_async_copy(x_any.at[:, 0:wc], xbuf, sems.at[4]),
        pltpu.make_async_copy(x_any.at[tokens - TAIL :, :], xtail, sems.at[5]),
        pltpu.make_async_copy(x_any.at[0:TAIL, :], xhead, sems.at[6]),
    ]
    if nch == 2:
        copies.append(pltpu.make_async_copy(x_any.at[:, wc:], last_ref, sems.at[12]))
    for copy in small + copies:
        copy.start()
    for copy in small:
        copy.wait()
    seg = seg_ref[...].astype(f32)
    seg_first = seg[:, 0:1]
    seg_last = [seg[:, (b + 1) * SPAN - 1 : (b + 1) * SPAN] for b in range(nb)]
    eye = iota((hp, hp), 0) == iota((hp, hp), 1)
    rate = jnp.exp(jnp.sum(jnp.where(eye, alog_ref[...], 0.0), axis=1, keepdims=True))
    skip = jnp.sum(jnp.where(eye, skip_ref[...], 0.0), axis=1, keepdims=True)
    dt = dt_ref[...]
    parts = split(dt * (rate * -LOG2E), 3)
    tri = jnp.where(iota((SPAN, SPAN), 0) <= iota((SPAN, SPAN), 1), 1.0, 0.0).astype(bf16)
    sums = mm(jnp.concatenate([parts[:, blk(b)] for b in range(nb)], 0), tri)
    lane = iota((hp, SPAN), 1)
    lane1 = iota((1, SPAN), 1)
    before = jnp.zeros((hp, 1), f32)
    kc = jnp.where(lane == 11, skip, 0.0)
    for b in range(nb):
        three = sums[3 * hp * b : 3 * hp * (b + 1)]
        cum = three[0:hp] + three[hp : 2 * hp] + three[2 * hp :]
        last = cum[:, SPAN - 1 : SPAN]
        segb, dtb = seg[:, blk(b)], dt[:, blk(b)]
        total = cum + before
        rows[0:hp, blk(b)] = cum
        rows[hp : 2 * hp, blk(b)] = jnp.exp2(total) * jnp.where(segb == seg_first, 1.0, 0.0)
        if b > 0:
            rows[2 * hp : 3 * hp, blk(b)] = jnp.exp2(cum) * jnp.where(segb == seg_last[b - 1], 1.0, 0.0)
            keep = jnp.exp2(last) * jnp.where(seg_last[b] == seg_last[b - 1], 1.0, 0.0)
            kc = kc + jnp.where(lane == b, keep, 0.0)
        else:
            rows[2 * hp : 3 * hp, blk(b)] = jnp.zeros((hp, SPAN), f32)
            is_drop = jnp.where((lane1 < KERNEL - 1) & (segb == seg_first), reached(1), 0.0)
            drop = jnp.sum(is_drop, axis=1, keepdims=True)
            early = jnp.exp2(jnp.where(lane < KERNEL - 1, -cum, 0.0)) * dtb * is_drop
            kc = kc + pltpu.roll(early, 8, 1)
        rows[3 * hp : 4 * hp, blk(b)] = jnp.exp2(last - cum) * dtb * jnp.where(segb == seg_last[b], 1.0, 0.0)
        rows[4 * hp : 5 * hp, blk(b)] = cum - jnp.log2(jnp.maximum(dtb, TINY))
        before = before + last
    fend = jnp.exp2(before) * jnp.where(seg_last[-1] == seg_first, 1.0, 0.0)
    kc = kc + jnp.where(lane == 0, fend, 0.0) + jnp.where(lane == 16, drop, 0.0)
    kcols[...] = kc
    delta = iota((SPAN, SPAN), 1) - iota((SPAN, SPAN), 0)
    edge = iota((TAIL, SPAN), 1) - iota((TAIL, SPAN), 0)
    for b in range(nb):
        segcol = to_column(seg[:, blk(b)])
        same = jnp.where(segcol == seg[:, blk(b)], 1.0, 0.0)
        if b > 0:
            past = jnp.concatenate([seg[:, b * SPAN - TAIL : b * SPAN], jnp.zeros((1, SPAN - TAIL), f32)], 1)
            same_past = jnp.where(segcol[0:TAIL] == past, 1.0, 0.0)
        for k in range(KERNEL - 1):
            back = KERNEL - 1 - k
            r = 3 * SPAN * b + SPAN * k
            shift[r : r + SPAN, :] = jnp.where(delta == -back, same, 0.0).astype(bf16)
            if b > 0:
                r = 3 * tokens + TAIL * (3 * b + k)
                shift[r : r + TAIL, :] = jnp.where(edge == TAIL - back, same_past, 0.0).astype(bf16)
    for copy in copies[:5]:
        copy.wait()
    bchead[:, 0:STATE] = bbuf[0:TAIL, :]
    bchead[:, STATE:] = craw[0:TAIL, :]
    every = slice(0, STATE)

    def keys():
        taps = taps_bc[:, 0:STATE] * 0.5
        for b in range(nb):
            bt[:, blk(b)] = conv_of(windows(shift, bbuf, b, every), bbuf[blk(b), :], taps).astype(bf16).T
            if nch == 1:
                queries(shift, craw, taps_bc, last_ref, b)

    chunk_state(
        hp, 0, xbuf, tapx[:, 0:wc] * 0.5, shift, bt, rows, kc, drop, xc, lstate, krows, msg, keys
    )
    for copy in copies[5:]:
        copy.wait()
    lane_last = iota((1, SPAN), 1)
    is_tail = jnp.where((lane_last >= SPAN - (KERNEL - 1)) & (seg[:, blk(nb - 1)] == seg_last[-1]), 1.0, 0.0)
    first_valid = 8.0 - jnp.sum(is_tail, axis=1, keepdims=True)

    def tail_of(value):
        rows8 = value.astype(f32)[8:16]
        return jnp.where(iota(rows8.shape, 0).astype(f32) >= first_valid, rows8, 0.0)

    tile0 = tail_of(xtail[:, 0:wc])
    if nch == 2:
        tile0 = tile0 + pltpu.roll(tail_of(xtail[:, wc:]), 4, 0)
    tail_b, tail_c = tail_of(bbuf[tokens - TAIL :, :]), tail_of(craw[tokens - TAIL :, :])
    if message_rows(wc) == STATE + 8:
        row0 = jnp.concatenate([tail_b[5:6], tail_c[5:6], tail_b[6:7], tail_c[6:7]], 1)
        mark = jnp.broadcast_to(seg_last[-1] + 1.0, (1, STATE))
        row4 = jnp.concatenate([tail_b[7:8], tail_c[7:8], mark, mark], 1)
        if wc > 4 * STATE:
            rest = jnp.zeros((1, wc - 4 * STATE), f32)
            row0, row4 = (jnp.concatenate([r, rest], 1) for r in (row0, row4))
        row = iota(tile0.shape, 0)
        tile0 = jnp.where(row == 0, row0, jnp.where(row == 4, row4, tile0))
        msg[STATE:, :] = tile0.astype(bf16)
        return
    tile0 = jnp.where(iota(tile0.shape, 0) == 0, seg_last[-1] + 1.0, tile0)
    tile1 = tail_b + pltpu.roll(tail_c, 4, 0)
    if wc > STATE:
        tile1 = jnp.concatenate([tile1, jnp.zeros((8, wc - STATE), f32)], 1)
    msg[STATE:, :] = jnp.concatenate([tile0, tile1], 0).astype(bf16)


def queries(shift, craw, taps_bc, cc, b):
    taps = taps_bc[:, STATE:] * 0.5
    sh = windows(shift, craw, b, slice(0, STATE))
    cc[blk(b), :] = conv_of(sh, craw[blk(b), :], taps).astype(bf16)


def next_kernel(
    hp, first, xbuf, tapx, shift, bt, rows, kcols, craw, taps_bc, msg, xc, lstate, krows, cc
):
    wc = xbuf.shape[1]

    def prepare():
        for b in range(xbuf.shape[0] // SPAN):
            queries(shift, craw, taps_bc, cc, b)

    chunk_state(
        hp, first, xbuf, tapx[:, wc : 2 * wc] * 0.5, shift, bt, rows, kcols[...],
        kcols[0:1, 16:17], xc, lstate, krows, msg, prepare,
    )


def early_conv(halo, head, taps):
    rows = jnp.concatenate([halo, head.astype(f32)[0:8]], 0)
    half = rows[5:13] * taps[0:1]
    for k in range(1, KERNEL):
        half = half + rows[5 + k : 13 + k] * taps[k : k + 1]
    return silu_from_half(half)


def relay_state(krows, recv, b8, xw8, flag):
    base = recv.astype(f32) * flag + mm(b8, xw8, 0, 0)
    return (base * krows[0:1]).astype(bf16)


def relay_first(nch, recv, xhead, bchead, tapx, taps_bc, seg_ref, cc, *refs):
    krows = refs[:nch]
    out, xw8_ref, x8_ref, b8_ref, c8_ref, flag_ref = refs[nch + 1 :]
    wc = out.shape[1]
    tile = recv[STATE:, :].astype(f32)
    tile0 = tile[0:8]
    mark = tile0[0:1, 0:1]
    if message_rows(wc) == STATE + 8:
        row = iota((8, STATE), 0)

        def three(at):
            first, second = tile0[0:1, at : at + STATE], tile0[0:1, at + 2 * STATE : at + 3 * STATE]
            third = jnp.where(row == 7, tile0[4:5, at : at + STATE], 0.0)
            return jnp.where(row == 5, first, jnp.where(row == 6, second, third))

        mark = tile0[4:5, 2 * STATE : 2 * STATE + 1]
        tail_b, tail_c = three(0), three(STATE)
    else:
        tail_b, tail_c = tile[8:16, 0:STATE], pltpu.roll(tile[8:16, 0:STATE], 4, 0)
    seg = seg_ref[:, 0:SPAN].astype(f32)
    seg_first = seg[:, 0:1]
    lane = iota((1, SPAN), 1)
    drop = jnp.sum(
        jnp.where((lane < KERNEL - 1) & (seg == seg_first), reached(1), 0.0), axis=1, keepdims=True
    )
    flag = jnp.where(mark == seg_first + 1.0, reached(1), 0.0)
    flag_ref[...] = jnp.broadcast_to(flag, (8, 128))

    def lower(value):
        return jnp.where(iota(value.shape, 0) >= 8 - (KERNEL - 1), value, 0.0) * flag

    def early(value):
        return jnp.where(iota(value.shape, 0).astype(f32) < drop, value, 0.0)

    zero8 = lambda n: jnp.zeros((8, n), f32)
    halo = [lower(tile0)]
    if nch == 2:
        halo.append(lower(pltpu.roll(tile0, 4, 0)))
    bc8 = early_conv(
        jnp.concatenate([lower(tail_b), lower(tail_c)], 1), bchead[...], taps_bc[...] * 0.5
    )
    b8 = jnp.concatenate([early(bc8[:, 0:STATE]), zero8(STATE)], 0).astype(bf16)
    b8_ref[...] = b8
    old = cc[0:TAIL, :].astype(f32)
    c8 = jnp.where(iota((8, STATE), 0).astype(f32) < drop, bc8[:, STATE:], old[0:8])
    c8_ref[...] = jnp.concatenate([c8, old[8:16]], 0).astype(bf16)
    for c in range(nch):
        cs = slice(c * wc, (c + 1) * wc)
        x8 = early(early_conv(halo[c], xhead[:, cs], tapx[:, cs] * 0.5)).astype(bf16).astype(f32)
        kr = krows[c][...]
        x8_ref[:, cs] = x8 * kr[11:12]
        xw8 = jnp.concatenate([x8 * kr[8:16], zero8(wc)], 0).astype(bf16)
        xw8_ref[:, cs] = xw8
        if c == 0:
            out[...] = relay_state(kr, recv[0:STATE, :], b8, xw8, flag)


def relay_next(recv, krows, b8, xw8, flag, out):
    wc = out.shape[1]
    out[...] = relay_state(krows[...], recv[...], b8[...], xw8[:, wc:], flag[0:1, 0:1])


def inflow_rhs(recv, xw8, flag):
    state = (recv[0:STATE, :].astype(f32) * flag[0:1, 0:1]).astype(bf16)
    return jnp.concatenate([state, xw8, jnp.zeros((128 - TAIL, state.shape[1]), bf16)], 0)


def local_kernel(hp, first, late, *refs):
    z_ref, xc, lstate, krows, cc, bt, rows, seg_ref = refs[:8]
    if late:
        cg, recv, xw8, x8, flag, order = refs[8:14]
    a_ref, q_ref = refs[-2:] if late else refs[-3:-1]
    tokens, wc = a_ref.shape
    nb = tokens // SPAN
    lane0 = first * HEAD_DIM
    lanes = slice(lane0, lane0 + wc)
    seg = seg_ref[...].astype(f32)
    ex = expander(hp, 2, wc, first)
    head_of = iota((128, SPAN), 0) & (hp - 1)
    low = iota((SPAN, 128), 1) < HEAD_DIM
    tri = iota((SPAN, SPAN), 0) >= iota((SPAN, SPAN), 1)
    if late:
        entering = inflow_rhs(recv, xw8[:, lanes], flag)
    for b in range(nb):
        segcol = to_column(seg[:, blk(b)])
        mask = (segcol == seg[:, blk(b)]) & tri
        c_blk = cc[blk(b), :]
        scores = jnp.where(mask, mm(c_blk, bt[:, blk(b)]), 0.0)
        scores = jnp.concatenate([scores, scores], 1)
        cum = split(rows[0:hp, blk(b)], 3)
        neg_q = split(-rows[4 * hp : 5 * hp, blk(b)], 3)
        ones = jnp.ones((3 * hp, SPAN), bf16)
        pad = jnp.zeros((128 - 6 * hp, SPAN), bf16)
        left = jnp.concatenate([cum, ones, pad], 0).T
        right = jnp.concatenate([ones, neg_q, pad], 0).astype(f32)
        f_exp = mm(split(rows[hp : 2 * hp, blk(b)], 2), ex, 0, 0)
        if late:
            inflow = mm(cg[blk(b), :], entering)
        if b > 0:
            e_exp = mm(split(rows[2 * hp : 3 * hp, blk(b)], 2), ex, 0, 0)
            carry = mm(c_blk, lstate[blk(b - 1), :])
        for j in range(wc // 128):
            js = slice(j * 128, (j + 1) * 128)
            xj = xc[blk(b), js]
            h = first + 2 * j
            sel = [jnp.where(head_of == h + i, right, 0.0).astype(bf16) for i in range(2)]
            decay = jnp.exp2(jnp.minimum(mm(left, jnp.concatenate(sel, 1)), 8.0))
            zero = jnp.zeros_like(xj)
            pair = jnp.concatenate([jnp.where(low, xj, zero), jnp.where(low, zero, xj)], 0)
            y = mm((scores * decay).astype(bf16), pair) + xj.astype(f32) * krows[11:12, js]
            if b > 0:
                y = y + e_exp[:, js] * carry[:, js]
            elif late:
                top = y[0:8] + x8[:, lane0 + j * 128 : lane0 + (j + 1) * 128]
                y = jnp.concatenate([top, y[8:]], 0)
            f = f_exp[:, js]
            if late:
                y = y + f * inflow[:, js]
            sz = silu_from_half(z_ref[blk(b), lane0 + j * 128 : lane0 + (j + 1) * 128].astype(f32) * 0.5)
            if b == 0 and not late:
                refs[-1][:, js] = sz[0:8]
            a_ref[blk(b), js] = y * sz
            q_ref[blk(b), js] = f * sz


def rank_kernel(cc, b8, c8, order, cg):
    tokens = cc.shape[0]
    b_pad = jnp.concatenate([b8[...], jnp.zeros((128 - TAIL, STATE), bf16)], 0)
    cg[:, 0:STATE] = cc[...]
    cg[0:TAIL, 0:STATE] = c8[...]
    g = mm(cg[:, 0:STATE], b_pad, 1, 1)
    causal = iota((tokens, 128), 0) >= iota((tokens, 128), 1)
    cg[:, STATE:] = jnp.where(causal, g, 0.0).astype(bf16)


def gate_kernel(nrecv, early, *refs):
    cg, flag, a_ref, q_ref, prev = refs[:5]
    recvs, refs = refs[5 : 5 + nrecv], refs[5 + nrecv :]
    gated, sums = refs[-2:]
    tokens, wc = a_ref.shape
    total = None
    if nrecv == 1:
        total = recvs[0][...]
    elif nrecv > 1:
        total = 0.0
        for i, r in enumerate(recvs):
            total = total + r[...].astype(f32) * reached(i + 2)
        total = total.astype(bf16)
    valid = flag[0:1, 0:1] * reached(2)
    if early:
        recv, xw8, x8, sz8 = refs[:4]
        entering = inflow_rhs(recv, xw8[:, 0:wc], flag)
    tile = min(256, wc)
    for b in range(tokens // SPAN):
        acc = None
        for j in range(wc // tile):
            js = slice(j * tile, (j + 1) * tile)
            g = a_ref[blk(b), js]
            if nrecv:
                g = g + (q_ref[blk(b), js] * valid) * mm(cg[blk(b), 0:STATE], total[:, js])
            if early:
                g = g + q_ref[blk(b), js] * mm(cg[blk(b), :], entering[:, js])
                if b == 0:
                    g = jnp.concatenate([g[0:8] + x8[:, js] * sz8[:, js], g[8:]], 0)
            gated[blk(b), js] = g
            sq = g * g
            for i in range(tile // 128):
                part = sq[:, i * 128 : (i + 1) * 128]
                acc = part if acc is None else acc + part
        sums[:, blk(b)] = prev[:, blk(b)] + jnp.sum(acc.T, axis=0, keepdims=True)


def norm_kernel(nch, sums, gain, *refs):
    gated, (out, buf, sems) = refs[:nch], refs[nch:]
    tokens, wc = gated[0].shape
    scale = lax.rsqrt(sums[...] / (HEADS * HEAD_DIM) + 1e-05)
    ones = jnp.ones((48, 128), bf16)
    copies = []
    for b in range(tokens // SPAN):
        wide = jnp.where(iota((16, SPAN), 0) == 0, scale[:, blk(b)], 0.0)
        col = mm(split(wide, 3), ones, 0, 0)
        for c in range(nch):
            for j in range(wc // 128):
                js = slice(j * 128, (j + 1) * 128)
                at = slice(c * wc + j * 128, c * wc + (j + 1) * 128)
                buf[blk(b), at] = (gated[c][blk(b), js] * col * gain[:, at]).astype(bf16)
        copy = pltpu.make_async_copy(buf.at[blk(b), :], out.at[blk(b), :], sems.at[b])
        copy.start()
        copies.append(copy)
    for copy in copies:
        copy.wait()


VMEM = pl.BlockSpec(memory_space=pltpu.VMEM)
ANY = pl.BlockSpec(memory_space=pl.ANY)


def call(body, ins, outs, scratch=(), name=None, limit=24 << 20):
    return pl.pallas_call(
        body,
        out_shape=[pltpu.VMEM(shape, dtype) for shape, dtype in outs],
        in_specs=ins,
        out_specs=[VMEM] * len(outs),
        scratch_shapes=list(scratch),
        compiler_params=pltpu.CompilerParams(vmem_limit_bytes=limit),
        name=name,
    )


def per_device(x_in, z_in, bc_in, conv_x, conv_bc, dt, a_log, skip_d, norm_gain, seg_ids):
    tokens, width = x_in.shape
    heads = dt.shape[0]
    nb = tokens // SPAN
    hp = max(16, heads)
    peers = lax.axis_size("seq")
    rounds = max(1, peers // 2)
    nch = 2 if width % 512 == 0 else 1
    wc = width // nch
    per_chunk = heads // nch
    members = lax.axis_size("head")

    def shift(value, hops):
        return lax.ppermute(value, ("seq", "head"), onward(peers, members, hops - 1))

    if hp != heads:
        dt = jnp.pad(dt, ((0, hp - heads), (0, 0)))
        a_log = jnp.pad(a_log, (0, hp - heads))
        skip_d = jnp.pad(skip_d, (0, hp - heads))
    seg = seg_ids.reshape(1, tokens)
    alog, skip = a_log.reshape(1, hp), skip_d.reshape(1, hp)
    state_outs = [((tokens, wc), bf16), ((SPAN * (nb - 1), wc), bf16), ((16, wc), f32)]
    dma = pltpu.SemaphoreType.DMA
    hbm = lambda value: pltpu.with_memory_space_constraint(value, pltpu.HBM)
    first = call(
        functools.partial(first_kernel, heads, hp, nch),
        [ANY] * 8,
        [((message_rows(wc), wc), bf16)] + state_outs
        + [
            ((STATE, tokens), bf16),
            ((5 * hp, tokens), f32),
            ((hp, 128), f32),
            ((3 * (tokens + TAIL * nb), SPAN), bf16),
            ((TAIL, width), bf16),
            ((TAIL, 2 * STATE), bf16),
            ((KERNEL, 2 * STATE), f32),
            ((KERNEL, width), f32),
            ((1, tokens), jnp.int32),
            ((tokens, STATE), bf16),
            ((tokens, wc if nch == 2 else STATE), bf16),
        ],
        [
            pltpu.VMEM((tokens, STATE), bf16),
            pltpu.VMEM((tokens, wc), bf16),
            pltpu.VMEM((TAIL, width), bf16),
            pltpu.VMEM((hp, tokens), f32),
            pltpu.VMEM((1, hp), f32),
            pltpu.VMEM((1, hp), f32),
            dma((13,)),
        ],
        name="first",
    )
    (
        msg, xc, ls, kr, bt, rows, kcols, shifts, xhead, bchead, taps_bc, tapx, seg, craw, cc
    ) = first(*[hbm(v) for v in (x_in, bc_in, conv_bc, conv_x, dt, alog, skip, seg)])
    xcs, lss, krs = [xc], [ls], [kr]
    recv1 = [shift(msg, 1)]
    if nch == 2:
        msg, xc, ls, kr, cc = call(
            functools.partial(next_kernel, hp, per_chunk),
            [VMEM] * 8,
            [((STATE, wc), bf16)] + state_outs + [((tokens, STATE), bf16)],
            name="next",
        )(cc, tapx, shifts, bt, rows, kcols, craw, taps_bc)
        xcs.append(xc)
        lss.append(ls)
        krs.append(kr)
        recv1.append(shift(msg, 1))
    def run_local(c, extra):
        late = len(extra) > 0
        outs = [((tokens, wc), f32)] * 2 + ([] if late else [((8, wc), f32)])
        return call(
            functools.partial(local_kernel, hp, c * per_chunk, late),
            [VMEM] * (8 + max(0, len(extra) - 1)) + [ANY] * late,
            outs,
            name=f"local{c}",
        )(z_in, xcs[c], lss[c], krs[c], cc, bt, rows, seg, *extra)

    local = [run_local(0, ())]
    relay, xw8, x8, b8, c8, flag = call(
        functools.partial(relay_first, nch),
        [VMEM] * (7 + nch) + [ANY],
        [
            ((STATE, wc), bf16),
            ((TAIL, width), bf16),
            ((8, width), f32),
            ((TAIL, STATE), bf16),
            ((TAIL, STATE), bf16),
            ((8, 128), f32),
        ],
        name="relay_first",
    )(recv1[0], xhead, bchead, tapx, taps_bc, seg, cc, *krs, local[0][2])
    later = [[] for c in range(nch)]
    if rounds > 1:
        later[0].append(shift(relay, 2))
    if nch == 2:
        (relay,) = call(relay_next, [VMEM] * 5, [((STATE, wc), bf16)], name="relay_next")(
            recv1[1], krs[1], b8, xw8, flag
        )
        if rounds > 1:
            later[1].append(shift(relay, 2))
    (cg,) = call(rank_kernel, [VMEM] * 3 + [ANY], [((tokens, 2 * STATE), bf16)], name="rank")(
        cc, b8, c8, relay
    )
    if nch == 2:
        local.append(run_local(1, (cg, recv1[1], xw8, x8, flag, relay)))
    for hops in range(3, rounds + 1):
        for c in range(nch):
            again = later[c][-1].astype(f32) * (krs[c][0:1] * flag[0:1, 0:1] * reached(hops - 1))
            later[c].append(shift(again.astype(bf16), hops))
    sums = jnp.zeros((1, tokens), f32)
    gated = []
    for c in range(nch):
        n = len(later[c])
        a, q, *rest = local[c]
        extra = [recv1[c], xw8, x8, *rest] if rest else []
        g, sums = call(
            functools.partial(gate_kernel, n, len(rest) > 0),
            [VMEM] * (5 + n + len(extra)),
            [((tokens, wc), f32), ((1, tokens), f32)],
            name=f"gate{c}",
        )(cg, flag, a, q, sums, *later[c], *extra)
        gated.append(g)
    swap = lambda step: lax.ppermute(sums, "head", [(i, i ^ step) for i in range(members)])
    step = 1
    while step < members:
        sums = sums + swap(step)
        step *= 2
    return pl.pallas_call(
        functools.partial(norm_kernel, nch),
        out_shape=jax.ShapeDtypeStruct((tokens, width), bf16),
        in_specs=[VMEM] * (2 + nch),
        out_specs=ANY,
        scratch_shapes=[pltpu.VMEM((tokens, width), bf16), dma((nb,))],
        compiler_params=pltpu.CompilerParams(vmem_limit_bytes=24 << 20),
        name="norm",
    )(sums, norm_gain.reshape(1, width), *gated)


def solution(mesh):
    in_specs = (
        P("seq", "head"),
        P("seq", "head"),
        P("seq", None),
        P(None, "head"),
        P(),
        P("head", "seq"),
        P("head"),
        P("head"),
        P("head"),
        P("seq"),
    )
    return jax.shard_map(
        per_device, mesh=mesh, in_specs=in_specs, out_specs=P("seq", "head"), check_vma=False
    )
```
